512 devices in a mesh: cfg: 2 (over core), req: 2 (over y_lo), seq: 128 (over z, x, y_hi).
Axes of the slice: x: 4, y: 8 (y_hi: 4, y_lo: 2; y = y_hi * 2 + y_lo), z: 8, core: 2. Of those that a mesh axis runs over, the one named last changes fastest.
Arguments:
- q_image: bfloat16 [2, 2048, 2048], P('cfg', ('req', 'seq')), parts along dimension 1, may hold values from -8 to 8
- k_image: bfloat16 [2, 2048, 2048], P('cfg', ('req', 'seq')), parts along dimension 1, may hold values from -8 to 8
- v_image: bfloat16 [2, 2048, 2048], P('cfg', ('req', 'seq')), parts along dimension 1, may hold values from -5 to 5
- k_text: bfloat16 [2, 1024, 2048], P('cfg', ('req', 'seq')), parts along dimension 1, may hold values from -6 to 6
- v_text: bfloat16 [2, 1024, 2048], P('cfg', ('req', 'seq')), parts along dimension 1, may hold values from -5 to 5
- text_len: int32 [2, 2], P('cfg', 'req'), parts along dimension 1, may hold values from 1 to 512
- shift: float32 [2, 2, 2048], P('cfg', 'req'), parts along dimension 1, may hold values from -1.5 to 1.5
- scale: float32 [2, 2, 2048], P('cfg', 'req'), parts along dimension 1, may hold values from -1.5 to 1.5
- w_latent: bfloat16 [2048, 64], replicated, may hold values from -0.125 to 0.125
- latents: float32 [2048, 64], P(('req', 'seq')), parts along dimension 0, may hold values from -1.2 to 1.2
- step_index: int32 [1], replicated, may hold values from 22 to 27
Outputs:
- latents_next: float32 [2048, 64], P(('req', 'seq'), 'cfg'), parts along dimension 0
- guided: float32 [2048, 64], P(('req', 'seq'), 'cfg'), parts along dimension 0
- norm: float32 [2], P('req'), parts along dimension 0
- max_logit: float32 [2, 2, 16], P('cfg', 'req'), parts along dimension 1
The draws below stay inside these ranges and needn't reach their ends.
There are 2 independent parts, one for each index of `req`. The reference program is written for one: setup_inputs(seed, part) draws one part's arguments, and reference() takes and returns one part's arrays. A program takes and returns all parts, laid end to end along the dimension named above; an argument that names none is the same for every part. Nothing has to cross between parts.
All inputs are finite; a program needn't handle non-finite values.
Results may differ from the reference program's by a relative error of at most 0.0062.
Values may be sent and summed in bfloat16 or wider, within the bound.
A program may use at most 64 MiB of HBM per device.

```python
import math
import jax
import jax.numpy as jnp
from jax import lax

TEXT = 512
HEADS = 16
HEAD_DIM = 128
CHAN = 64
STEPS = 28
IMAGE = 1024
FEAT = 2048


def base_field(key, shape):
    return jax.random.truncated_normal(key, -4.0, 4.0, shape, jnp.float32)


def paired_copies(key, salt, rows, spread):
    pair_key = jax.random.fold_in(key, salt)
    first_key, fresh_key = jax.random.split(pair_key)
    shape = (rows, HEADS * HEAD_DIM)
    first = base_field(first_key, shape)
    fresh = base_field(fresh_key, shape)
    second = 0.99 * first + 0.14 * fresh
    return spread * jnp.stack([first, second])


def aligned_pair(key):
    base_key = jax.random.fold_in(key, 11)
    query_key, other_key, pick_key, count_key = jax.random.split(base_key, 4)
    shape = (IMAGE, HEADS * HEAD_DIM)
    first_q = base_field(query_key, shape)
    other_q = base_field(other_key, shape)
    segment_rows = IMAGE // 8
    order = jax.random.permutation(pick_key, 8)
    count = jax.random.randint(count_key, (), 3, 6)
    row_shared = jnp.repeat(order < count, segment_rows)
    second_q = jnp.where(row_shared[:, None], first_q, other_q)
    queries = 1.3 * jnp.stack([first_q, second_q])
    keys_drawn = paired_copies(key, 31, IMAGE, 1.3)
    return (queries, keys_drawn)


def draw_q_image(key, part):
    return aligned_pair(key)[0].astype(jnp.bfloat16)


def draw_k_image(key, part):
    return aligned_pair(key)[1].astype(jnp.bfloat16)


def draw_v_image(key, part):
    return paired_copies(key, 41, IMAGE, 1.0).astype(jnp.bfloat16)


def draw_k_text(key, part):
    return paired_copies(key, 43, TEXT, 1.3).astype(jnp.bfloat16)


def draw_v_text(key, part):
    return paired_copies(key, 47, TEXT, 1.0).astype(jnp.bfloat16)


def draw_latents(key, part):
    noise_key = jax.random.fold_in(key, 23)
    value_key, row_key, col_key = jax.random.split(noise_key, 3)
    ramp = jnp.arange(IMAGE, dtype=jnp.float32)[:, None] / IMAGE
    row_scale = jnp.exp(jax.random.uniform(row_key, (IMAGE, 1), jnp.float32, jnp.log(0.006), jnp.log(0.08)))
    col_scale = jnp.exp(jax.random.uniform(col_key, (1, CHAN), jnp.float32, jnp.log(0.4), jnp.log(1.2)))
    values = jax.random.truncated_normal(value_key, -4.0, 4.0, (IMAGE, CHAN), jnp.float32)
    return values * row_scale * col_scale * jnp.exp(jnp.log(3.0) * ramp)


def block_levels(stream_key, extent, shards, low, largest):
    level, own = 1.0, jax.random.fold_in(stream_key, 6)
    for dim, blocks in shards:
        heights = jnp.exp(jax.random.uniform(jax.random.fold_in(own, dim), (blocks,), jnp.float32, low / len(shards), largest / len(shards)))
        level = level * jnp.repeat(heights, extent[dim] // blocks).reshape([-1 if axis == dim else 1 for axis in range(len(extent))])
    return level


def scatter_about(own_key, extent, deviation, limit, shards=(), kind=jnp.bfloat16):
    values = deviation * jax.random.normal(own_key, extent, jnp.float32)
    if shards:
        values = values * block_levels(own_key, extent, shards, -0.22, 0.18)
    return jnp.clip(values, -limit, limit).astype(kind)


def setup_inputs(seed: int = 0, part: int = 0) -> dict:
    key_list = jax.random.split(jax.random.key(seed), 12)
    part_splits = jax.random.split(jax.random.fold_in(key_list[11], part), 12)
    q_image = draw_q_image(jax.random.fold_in(jax.random.fold_in(key_list[11], part), 71), part)
    k_image = draw_k_image(jax.random.fold_in(jax.random.fold_in(key_list[11], part), 71), part)
    v_image = draw_v_image(jax.random.fold_in(jax.random.fold_in(key_list[11], part), 71), part)
    k_text = draw_k_text(jax.random.fold_in(jax.random.fold_in(key_list[11], part), 71), part)
    v_text = draw_v_text(jax.random.fold_in(jax.random.fold_in(key_list[11], part), 71), part)
    text_len = jax.random.randint(part_splits[5], (2, 1), 1, TEXT + 1).astype(jnp.int32)
    shift = scatter_about(part_splits[6], (2, 1, FEAT), 0.25, 1.5, ((0, 2),), jnp.float32)
    scale = scatter_about(part_splits[7], (2, 1, FEAT), 0.3, 1.5, ((0, 2),), jnp.float32)
    w_latent = scatter_about(key_list[8], (FEAT, CHAN), FEAT ** -0.5, 0.125)
    latents = draw_latents(jax.random.fold_in(jax.random.fold_in(key_list[11], part), 71), part)
    step_index = jax.random.randint(key_list[10], (1,), STEPS - 6, STEPS).astype(jnp.int32)
    return dict(q_image=q_image, k_image=k_image, v_image=v_image, k_text=k_text, v_text=v_text, text_len=text_len, shift=shift, scale=scale, w_latent=w_latent, latents=latents, step_index=step_index)


GUIDANCE = 3.5
SIGMA_SHIFT = 3.0

def sigma_at(position):
    level = 1.0 - position.astype(jnp.float32) / STEPS
    return SIGMA_SHIFT * level / (1.0 + (SIGMA_SHIFT - 1.0) * level)

def attend_block(queries, all_keys, all_values, usable, inv_root):
    scores = jnp.einsum('qhd,khd->hqk', queries, all_keys) * inv_root
    scores = jnp.where(usable[None, None, :], scores, -jnp.inf)
    row_peak = lax.optimization_barrier(jnp.max(scores, axis=-1))
    weights = jnp.exp(scores - row_peak[:, :, None]).astype(jnp.bfloat16)
    weight_sum = lax.optimization_barrier(jnp.sum(weights.astype(jnp.float32), axis=-1))
    summed = jnp.einsum('hqk,khd->qhd', weights.astype(jnp.float32), all_values)
    attended = (summed / jnp.transpose(weight_sum)[:, :, None]).astype(jnp.bfloat16)
    return (attended, lax.optimization_barrier(jnp.max(row_peak, axis=1)))

def reference(q_image, k_image, v_image, k_text, v_text, text_len, shift, scale, w_latent, latents, step_index):
    block_rows = min(512, IMAGE)
    inv_root = 1.0 / math.sqrt(HEAD_DIM)
    velocities = []
    peaks = []
    for copy_index in range(2):
        queries = q_image[copy_index].astype(jnp.float32).reshape(IMAGE // block_rows, block_rows, HEADS, HEAD_DIM)
        all_keys = jnp.concatenate([k_image[copy_index], k_text[copy_index]], axis=0).astype(jnp.float32).reshape(-1, HEADS, HEAD_DIM)
        all_values = jnp.concatenate([v_image[copy_index], v_text[copy_index]], axis=0).astype(jnp.float32).reshape(-1, HEADS, HEAD_DIM)
        text_pos = jnp.arange(TEXT, dtype=jnp.int32)
        usable = jnp.concatenate([jnp.ones((IMAGE,), dtype=bool), text_pos < text_len[copy_index, 0]])

        def one_block(query_block):
            return attend_block(query_block, all_keys, all_values, usable, inv_root)
        outputs, maxima = lax.map(one_block, queries)
        attended = outputs.reshape(IMAGE, FEAT)
        peaks.append(lax.optimization_barrier(jnp.max(maxima, axis=0)))
        features = attended.astype(jnp.float32)
        average = lax.optimization_barrier(jnp.mean(features, axis=1, keepdims=True))
        centered = features - average
        variance = lax.optimization_barrier(jnp.mean(centered * centered, axis=1, keepdims=True))
        normed = (centered * lax.rsqrt(variance + 1e-06) * (1.0 + scale[copy_index, 0]) + shift[copy_index, 0]).astype(jnp.bfloat16)
        velocities.append(jnp.dot(normed, w_latent, preferred_element_type=jnp.float32))
    guided = velocities[1] + GUIDANCE * (velocities[0] - velocities[1])
    delta = sigma_at(step_index[0] + 1) - sigma_at(step_index[0])
    latents_next = latents + delta * guided
    norm = jnp.sqrt(jnp.sum(latents_next * latents_next) / (IMAGE * CHAN)).reshape(1)
    max_logit = jnp.stack(peaks).reshape(2, 1, HEADS)
    return (latents_next, guided, norm, max_logit)
```

```python
import math

import jax
import jax.numpy as jnp
from jax import lax
from jax.experimental import pallas as pl
from jax.experimental.pallas import tpu as pltpu
from jax.sharding import PartitionSpec as P

HEADS = 16
HEAD_DIM = 128
FEAT = HEADS * HEAD_DIM
CHAN = 64
STEPS = 28
GUIDANCE = 3.5
SIGMA_SHIFT = 3.0

NZ, NX, NY = 8, 4, 4
SEQ = NZ * NX * NY
ROWS = 8
TROWS = 4
OWNERS = NZ * NX
QROWS = OWNERS * ROWS
UNITS = HEADS * NY
FAR_4 = (2, 1, 3, 0)

MESH = pl.DeviceIdType.MESH
BF16 = jnp.bfloat16
F32 = jnp.float32


def remote(src, dst, send_sem, recv_sem, device):
    return pltpu.make_async_remote_copy(
        src_ref=src,
        dst_ref=dst,
        send_sem=send_sem,
        recv_sem=recv_sem,
        device_id=device,
        device_id_type=MESH,
    )


def wait_bytes(ref, sem):
    pltpu.make_async_copy(ref, ref, sem).wait()


def nt_dot(a, b):
    return lax.dot_general(a, b, (((1,), (1,)), ((), ())), preferred_element_type=F32)


def sigma_at(position):
    level = 1.0 - position / STEPS
    return SIGMA_SHIFT * level / (1.0 + (SIGMA_SHIFT - 1.0) * level)


def far_first(i):
    return NZ // 2 + ((i + 1) // 2) * (1 - 2 * lax.rem(i, 2))


def over_z(body):
    def step(i, carry):
        body(far_first(i), False)
        return carry

    lax.fori_loop(0, NZ - 1, step, 0)
    body(0, True)


def kernel(
    len_ref,
    step_ref,
    q_hbm,
    k_hbm,
    v_hbm,
    kt_hbm,
    vt_hbm,
    shift_hbm,
    scale_hbm,
    w_hbm,
    lat_hbm,
    lat_out,
    guided_out,
    norm_out,
    peak_out,
    q_own,
    k_own,
    v_own,
    kt_own,
    vt_own,
    w_own,
    lat_own,
    mod,
    q_send,
    k_send,
    t_send,
    v_send,
    q_all,
    k_all,
    t_all,
    v_all,
    att,
    peak_row,
    heads_in,
    sums,
    local_sem,
    send_sem,
    recv_sem,
):
    cfg = lax.axis_index("cfg")
    me = lax.axis_index("seq")
    other = 1 - cfg
    z = me // (NX * NY)
    x = lax.rem(me // NY, NX)
    y = lax.rem(me, NY)
    attends = lax.rem(z + x, 2) == cfg
    idle = lax.rem(z + x, 2) != cfg
    my_head = z * 2 + x // 2
    my_slot = z * NX + x
    xs = [lax.rem(x + d, NX) for d in FAR_4]
    ys = [lax.rem(y + d, NY) for d in FAR_4]
    plane = [xx * NY + yy for xx in xs for yy in ys]

    loads = [
        (q_hbm.at[0], q_own),
        (k_hbm.at[0], k_own),
        (kt_hbm.at[0], kt_own),
        (vt_hbm.at[0], vt_own),
        (v_hbm.at[0], v_own),
        (shift_hbm.at[0], mod.at[cfg, 0]),
        (scale_hbm.at[0], mod.at[cfg, 1]),
        (w_hbm, w_own),
        (lat_hbm, lat_own),
    ]
    copies = [pltpu.make_async_copy(s, d, local_sem.at[i]) for i, (s, d) in enumerate(loads)]
    for copy in copies:
        copy.start()

    barrier = pltpu.get_barrier_semaphore()

    def greet(device):
        pl.semaphore_signal(barrier, inc=1, device_id=device, device_id_type=MESH)

    greet({"cfg": other, "seq": me})

    @pl.when(attends)
    def _():
        def signals(dz, here):
            base = lax.rem(z + dz, NZ) * (NX * NY)
            for offset in plane[:-1] if here else plane:
                greet({"cfg": cfg, "seq": base + offset})

        over_z(signals)

    for copy in copies:
        copy.wait()
    for h in range(HEADS):
        cols = slice(h * HEAD_DIM, (h + 1) * HEAD_DIM)
        q_send[h] = q_own[:, cols]
        k_send[h] = k_own[:, cols]
        t_send[h, 0] = kt_own[:, cols]
        t_send[h, 1] = vt_own[:, cols]
        v_send[h] = v_own[:, cols]

    @pl.when(attends)
    def _():
        pl.semaphore_wait(barrier, UNITS)

    @pl.when(idle)
    def _():
        pl.semaphore_wait(barrier, UNITS + 1)

    def to_units(pieces):
        def sends(dz, here):
            zz = lax.rem(z + dz, NZ)
            parity = lax.rem(zz + cfg, 2)
            base = (zz * NX + parity) * NY
            for dy, yy in zip(FAR_4, ys):
                for half in range(2):
                    head = zz * 2 + half
                    unit = base + (2 * half * NY + yy)

                    def away():
                        for i, src, dst in pieces(head, dy == 0):
                            device = {"cfg": cfg, "seq": unit}
                            remote(src, dst, send_sem.at[i], recv_sem.at[i], device).start()

                    def local():
                        for i, src, dst in pieces(head, True):
                            pltpu.make_async_copy(src, dst, recv_sem.at[i]).start()

                    if here and dy == 0:
                        pl.when(2 * half + parity != x)(away)
                        pl.when(2 * half + parity == x)(local)
                    else:
                        away()

        over_z(sends)

    def keys(head, own_block):
        parts = [(0, k_send.at[head], k_all.at[me]), (1, t_send.at[head], t_all.at[me])]
        if own_block:
            parts.append((2, q_send.at[head], q_all.at[my_slot]))
        return parts

    to_units(keys)
    to_units(lambda head, own_block: [(3, v_send.at[head], v_all.at[me])])

    mod_copy = remote(
        mod.at[cfg], mod.at[cfg], send_sem.at[4], recv_sem.at[4], {"cfg": other, "seq": me}
    )
    mod_copy.start()
    lane = lax.broadcasted_iota(jnp.int32, (1, HEAD_DIM), 1)
    peak_row[...] = jnp.full((1, HEAD_DIM), -jnp.inf)

    @pl.when(attends)
    def _():
        wait_bytes(k_all, recv_sem.at[0])
        wait_bytes(t_all, recv_sem.at[1])
        wait_bytes(q_all, recv_sem.at[2])
        inv_root = 1.0 / math.sqrt(HEAD_DIM)
        rate = inv_root * math.log2(math.e)
        q = q_all[...].reshape(QROWS, HEAD_DIM)
        image = nt_dot(q, k_all[...].reshape(SEQ * ROWS, HEAD_DIM))
        text = nt_dot(q, t_all[:, 0].reshape(SEQ * TROWS, HEAD_DIM))
        position = lax.broadcasted_iota(jnp.int32, (1, SEQ * TROWS), 1)
        text = jnp.where(position < len_ref[...], text, -jnp.inf)
        peak = jnp.maximum(
            jnp.max(image, axis=1, keepdims=True), jnp.max(text, axis=1, keepdims=True)
        )
        image = jnp.exp2((image - peak) * rate).astype(BF16)
        text = jnp.exp2((text - peak) * rate).astype(BF16)
        top = jnp.max(peak, axis=0, keepdims=True) * inv_root
        peak_row[...] = jnp.where(lane == my_head, top, -jnp.inf)
        wait_bytes(v_all, recv_sem.at[3])
        ones = jnp.ones((SEQ * ROWS, HEAD_DIM), BF16)
        v_image = jnp.concatenate([v_all[...].reshape(SEQ * ROWS, HEAD_DIM), ones], axis=1)
        v_text = jnp.concatenate(
            [t_all[:, 1].reshape(SEQ * TROWS, HEAD_DIM), ones[: SEQ * TROWS]], axis=1
        )
        summed = jnp.dot(image, v_image, preferred_element_type=F32) + jnp.dot(
            text, v_text, preferred_element_type=F32
        )
        result = (summed[:, :HEAD_DIM] / summed[:, HEAD_DIM:]).astype(BF16)
        att[...] = result.reshape(OWNERS, ROWS, HEAD_DIM)

        def give(dz, here):
            base = lax.rem(z + dz, NZ) * NX
            for dx, xx in zip(FAR_4, xs):
                slot = base + xx
                dst = heads_in.at[cfg, my_head]
                owner = slot * NY + y
                remote(
                    att.at[slot], dst, send_sem.at[5], recv_sem.at[5], {"cfg": other, "seq": owner}
                ).start()
                if here and dx == 0:
                    pltpu.make_async_copy(att.at[slot], dst, recv_sem.at[5]).start()
                else:
                    remote(
                        att.at[slot], dst, send_sem.at[5], recv_sem.at[5], {"cfg": cfg, "seq": owner}
                    ).start()

        over_z(give)

    mod_copy.wait_recv()
    wait_bytes(heads_in, recv_sem.at[5])
    parts = heads_in[...].astype(F32)
    average = jnp.sum(jnp.sum(parts, axis=1, keepdims=True), axis=3, keepdims=True) / FEAT
    parts = parts - average
    squares = jnp.sum(parts * parts, axis=1, keepdims=True)
    variance = jnp.sum(squares, axis=3, keepdims=True) / FEAT
    factor = lax.rsqrt(variance + 1e-06)
    normed = (parts * factor * (1.0 + mod[:, 1]) + mod[:, 0]).astype(BF16)
    normed = jnp.concatenate([normed[:, h] for h in range(HEADS)], axis=2)
    velocity = nt_dot(normed.reshape(2 * ROWS, FEAT), w_own[...])
    uncond = velocity[ROWS:]
    guided = uncond + GUIDANCE * (velocity[:ROWS] - uncond)
    position = jnp.broadcast_to(step_ref[...].astype(F32), (1, CHAN))
    delta = sigma_at(position + 1.0) - sigma_at(position)
    latents = lat_own[...] + delta * guided
    square = jnp.sum(
        jnp.sum(latents * latents, axis=1, keepdims=True), axis=0, keepdims=True
    )
    sums[me] = jnp.where(lane == HEADS, square, peak_row[...])

    def share(dz, here):
        base = lax.rem(z + dz, NZ) * (NX * NY)
        for offset in plane[:-1] if here else plane:
            remote(
                sums.at[me],
                sums.at[me],
                send_sem.at[6],
                recv_sem.at[6],
                {"cfg": cfg, "seq": base + offset},
            ).start()

    over_z(share)

    half = CHAN // 2
    lat_out[...] = jnp.where(cfg == 0, latents[:, :half], latents[:, half:])
    guided_out[...] = jnp.where(cfg == 0, guided[:, :half], guided[:, half:])

    mod_copy.wait_send()

    @pl.when(attends)
    def _():
        wait_bytes(k_all.at[: UNITS - 1], send_sem.at[0])
        wait_bytes(t_all.at[: UNITS - 1], send_sem.at[1])
        wait_bytes(q_all.at[: HEADS - 1], send_sem.at[2])
        wait_bytes(v_all.at[: UNITS - 1], send_sem.at[3])
        wait_bytes(k_all.at[: 2 * OWNERS - 1], send_sem.at[5])

    @pl.when(idle)
    def _():
        wait_bytes(k_all.at[:UNITS], send_sem.at[0])
        wait_bytes(t_all.at[:UNITS], send_sem.at[1])
        wait_bytes(q_all.at[:HEADS], send_sem.at[2])
        wait_bytes(v_all.at[:UNITS], send_sem.at[3])

    wait_bytes(sums.at[: SEQ - 1], recv_sem.at[6])
    wait_bytes(sums.at[: SEQ - 1], send_sem.at[6])
    rows = sums[...]
    norm = jnp.sqrt(jnp.sum(rows, axis=0) / (SEQ * ROWS * CHAN))
    norm_out[...] = norm[:, HEADS : HEADS + 1]
    peak_out[...] = jnp.max(rows, axis=0)[:, :HEADS]


def hand_over(*refs):
    sem = refs[8]
    copies = [pltpu.make_async_copy(refs[i], refs[4 + i], sem.at[i]) for i in range(4)]
    for copy in copies:
        copy.start()
    for copy in copies:
        copy.wait()


def per_device(
    q_image, k_image, v_image, k_text, v_text, text_len, shift, scale, w_latent, latents, step_index
):
    anywhere = pl.BlockSpec(memory_space=pltpu.HBM)
    vmem = pl.BlockSpec(memory_space=pltpu.VMEM)
    half = CHAN // 2
    shapes = [
        jax.ShapeDtypeStruct((ROWS, half), F32),
        jax.ShapeDtypeStruct((ROWS, half), F32),
        jax.ShapeDtypeStruct((1, 1), F32),
        jax.ShapeDtypeStruct((1, HEADS), F32),
    ]
    results = pl.pallas_call(
        kernel,
        out_shape=shapes,
        in_specs=[vmem] * 2 + [anywhere] * 9,
        out_specs=[vmem] * 4,
        scratch_shapes=[
            pltpu.VMEM((ROWS, FEAT), BF16),
            pltpu.VMEM((ROWS, FEAT), BF16),
            pltpu.VMEM((ROWS, FEAT), BF16),
            pltpu.VMEM((TROWS, FEAT), BF16),
            pltpu.VMEM((TROWS, FEAT), BF16),
            pltpu.VMEM((CHAN, FEAT), BF16),
            pltpu.VMEM((ROWS, CHAN), F32),
            pltpu.VMEM((2, 2, HEADS, 1, HEAD_DIM), F32),
            pltpu.VMEM((HEADS, ROWS, HEAD_DIM), BF16),
            pltpu.VMEM((HEADS, ROWS, HEAD_DIM), BF16),
            pltpu.VMEM((HEADS, 2, TROWS, HEAD_DIM), BF16),
            pltpu.VMEM((HEADS, ROWS, HEAD_DIM), BF16),
            pltpu.VMEM((OWNERS, ROWS, HEAD_DIM), BF16),
            pltpu.VMEM((SEQ, ROWS, HEAD_DIM), BF16),
            pltpu.VMEM((SEQ, 2, TROWS, HEAD_DIM), BF16),
            pltpu.VMEM((SEQ, ROWS, HEAD_DIM), BF16),
            pltpu.VMEM((OWNERS, ROWS, HEAD_DIM), BF16),
            pltpu.VMEM((1, HEAD_DIM), F32),
            pltpu.VMEM((2, HEADS, ROWS, HEAD_DIM), BF16),
            pltpu.VMEM((SEQ, 1, HEAD_DIM), F32),
            pltpu.SemaphoreType.DMA((9,)),
            pltpu.SemaphoreType.DMA((7,)),
            pltpu.SemaphoreType.DMA((7,)),
        ],
        compiler_params=pltpu.CompilerParams(collective_id=0, has_side_effects=True),
        name="joint_attention_step",
    )(
        text_len,
        step_index.reshape(1, 1),
        q_image,
        k_image,
        v_image,
        k_text,
        v_text,
        shift.reshape(1, HEADS, 1, HEAD_DIM),
        scale.reshape(1, HEADS, 1, HEAD_DIM),
        w_latent.T,
        latents,
    )
    latents_half, guided_half, norm, peaks = pl.pallas_call(
        hand_over,
        out_shape=shapes,
        in_specs=[anywhere] * 4,
        out_specs=[anywhere] * 4,
        scratch_shapes=[pltpu.SemaphoreType.DMA((4,))],
        name="hand_over",
    )(*results)
    return (latents_half, guided_half, norm.reshape(1), peaks.reshape(1, 1, HEADS))


def solution(mesh):
    placed = (
        P("cfg", ("req", "seq"), None),
        P("cfg", ("req", "seq"), None),
        P("cfg", ("req", "seq"), None),
        P("cfg", ("req", "seq"), None),
        P("cfg", ("req", "seq"), None),
        P("cfg", "req"),
        P("cfg", "req", None),
        P("cfg", "req", None),
        P(),
        P(("req", "seq"), None),
        P(),
    )
    return jax.shard_map(
        per_device,
        mesh=mesh,
        in_specs=placed,
        out_specs=(
            P(("req", "seq"), "cfg"),
            P(("req", "seq"), "cfg"),
            P("req"),
            P("cfg", "req", None),
        ),
        check_vma=False,
    )
```

```python
import math

import jax
import jax.numpy as jnp
from jax import lax
from jax.experimental import pallas as pl
from jax.experimental.pallas import tpu as pltpu
from jax.sharding import PartitionSpec as P

HEADS = 16
HEAD_DIM = 128
FEAT = HEADS * HEAD_DIM
CHAN = 64
STEPS = 28
GUIDANCE = 3.5
SIGMA_SHIFT = 3.0

NZ, NX, NY = 8, 4, 4
SEQ = NZ * NX * NY
ROWS = 8
TROWS = 4
UZ = HEADS // NX
BLOCKS = 2
QY = NY // BLOCKS
OWNERS = NZ * NX * QY
CHUNK = 16
UNITS = HEADS * BLOCKS
FAR_4 = (2, 1, 3, 0)

MESH = pl.DeviceIdType.MESH
BF16 = jnp.bfloat16
F32 = jnp.float32


def remote(src, dst, send_sem, recv_sem, device):
    return pltpu.make_async_remote_copy(
        src_ref=src,
        dst_ref=dst,
        send_sem=send_sem,
        recv_sem=recv_sem,
        device_id=device,
        device_id_type=MESH,
    )


def wait_bytes(ref, sem):
    pltpu.make_async_copy(ref, ref, sem).wait()


def nt_dot(a, b):
    return lax.dot_general(a, b, (((1,), (1,)), ((), ())), preferred_element_type=F32)


def sigma_at(position):
    level = 1.0 - position / STEPS
    return SIGMA_SHIFT * level / (1.0 + (SIGMA_SHIFT - 1.0) * level)


def far_first(i):
    return NZ // 2 + ((i + 1) // 2) * (1 - 2 * lax.rem(i, 2))


def unit_y(z, x, block, cfg):
    return block if QY == 1 else block * QY + lax.rem(z + x + cfg, QY)


def over_z(body):
    def step(i, carry):
        body(far_first(i), False)
        return carry

    lax.fori_loop(0, NZ - 1, step, 0)
    body(0, True)


def kernel(
    len_ref,
    step_ref,
    q_hbm,
    k_hbm,
    v_hbm,
    kt_hbm,
    vt_hbm,
    shift_hbm,
    scale_hbm,
    w_hbm,
    lat_hbm,
    out_ref,
    w_own,
    lat_own,
    mod,
    q_all,
    k_all,
    kt_all,
    v_all,
    vt_all,
    att,
    peak_row,
    heads_in,
    sums,
    local_sem,
    send_sem,
    recv_sem,
):
    cfg = lax.axis_index("cfg")
    me = lax.axis_index("seq")
    other = 1 - cfg
    z = me // (NX * NY)
    x = lax.rem(me // NY, NX)
    y = lax.rem(me, NY)
    block = y // QY
    attends = (z < UZ) & (y == unit_y(z, x, block, cfg))
    idle = jnp.logical_not(attends)
    my_head = z * NX + x
    my_slot = (z * NX + x) * QY + lax.rem(y, QY)
    xs = [lax.rem(x + d, NX) for d in FAR_4]
    ys = [lax.rem(y + d, NY) for d in FAR_4]
    plane = [xx * NY + yy for xx in xs for yy in ys]

    loads = [
        (shift_hbm.at[0], mod.at[cfg, 0]),
        (scale_hbm.at[0], mod.at[cfg, 1]),
        (w_hbm, w_own),
        (lat_hbm, lat_own),
    ]
    copies = [pltpu.make_async_copy(s, d, local_sem.at[i]) for i, (s, d) in enumerate(loads)]
    for copy in copies:
        copy.start()

    barrier = pltpu.get_barrier_semaphore()

    def greet(device):
        pl.semaphore_signal(barrier, inc=1, device_id=device, device_id_type=MESH)

    greet({"cfg": other, "seq": me})

    @pl.when(attends)
    def _():
        def signals(dz, here):
            base = lax.rem(z + dz, NZ) * (NX * NY)
            for offset in plane[:-1] if here else plane:
                greet({"cfg": cfg, "seq": base + offset})

        over_z(signals)

    @pl.when(attends)
    def _():
        pl.semaphore_wait(barrier, UNITS)

    @pl.when(idle)
    def _():
        pl.semaphore_wait(barrier, UNITS + 1)

    def to_units(pieces):
        def sends(zz, here):
            for dx, xx in zip(FAR_4, xs):
                head = zz * NX + xx
                for db in reversed(range(BLOCKS)):
                    unit = head * NY + unit_y(zz, xx, lax.rem(block + db, BLOCKS), cfg)

                    def away():
                        for i, src, dst in pieces(head, db == 0):
                            device = {"cfg": cfg, "seq": unit}
                            remote(src, dst, send_sem.at[i], recv_sem.at[i], device).start()

                    def local():
                        for i, src, dst in pieces(head, True):
                            pltpu.make_async_copy(src, dst, recv_sem.at[i]).start()

                    if here and dx == 0 and db == 0:
                        pl.when(unit != me)(away)
                        pl.when(unit == me)(local)
                    else:
                        away()

        def step(i, carry):
            sends(lax.rem(z + 1 + i, UZ), False)
            return carry

        lax.fori_loop(0, UZ - 1, step, 0)
        sends(lax.rem(z, UZ), True)

    def slice_of(ref, head):
        return ref.at[0, :, pl.ds(pl.multiple_of(head * HEAD_DIM, HEAD_DIM), HEAD_DIM)]

    def keys(head, own_block):
        parts = [
            (0, slice_of(k_hbm, head), k_all.at[me]),
            (1, slice_of(kt_hbm, head), kt_all.at[me]),
        ]
        if own_block:
            parts.append((2, slice_of(q_hbm, head), q_all.at[my_slot]))
        return parts

    def values(head, own_block):
        return [
            (3, slice_of(v_hbm, head), v_all.at[me]),
            (7, slice_of(vt_hbm, head), vt_all.at[me]),
        ]

    to_units(keys)
    to_units(values)

    for copy in copies:
        copy.wait()
    mod_copy = remote(
        mod.at[cfg], mod.at[cfg], send_sem.at[4], recv_sem.at[4], {"cfg": other, "seq": me}
    )
    mod_copy.start()
    lane = lax.broadcasted_iota(jnp.int32, (1, HEAD_DIM), 1)
    peak_row[...] = jnp.full((1, HEAD_DIM), -jnp.inf)

    @pl.when(attends)
    def _():
        wait_bytes(k_all, recv_sem.at[0])
        wait_bytes(kt_all, recv_sem.at[1])
        wait_bytes(q_all, recv_sem.at[2])
        inv_root = 1.0 / math.sqrt(HEAD_DIM)
        rate = inv_root * math.log2(math.e)
        keys_image = k_all[...].reshape(SEQ * ROWS, HEAD_DIM)
        keys_text = kt_all[...].reshape(SEQ * TROWS, HEAD_DIM)
        position = lax.broadcasted_iota(jnp.int32, (1, SEQ * TROWS), 1)
        usable = position < len_ref[...]
        weights = []
        top = None
        for start in range(0, OWNERS, CHUNK):
            q = q_all[start : start + CHUNK].reshape(CHUNK * ROWS, HEAD_DIM)
            image = nt_dot(q, keys_image)
            text = jnp.where(usable, nt_dot(q, keys_text), -jnp.inf)
            peak = jnp.maximum(
                jnp.max(image, axis=1, keepdims=True), jnp.max(text, axis=1, keepdims=True)
            )
            image = jnp.exp2((image - peak) * rate).astype(BF16)
            text = jnp.exp2((text - peak) * rate).astype(BF16)
            weights.append((image, text))
            most = jnp.max(peak, axis=0, keepdims=True)
            top = most if top is None else jnp.maximum(top, most)
        peak_row[...] = jnp.where(lane == my_head, top * inv_root, -jnp.inf)
        ones = jnp.ones((SEQ * ROWS, HEAD_DIM), BF16)
        wait_bytes(v_all, recv_sem.at[3])
        wait_bytes(vt_all, recv_sem.at[7])
        v_image = jnp.concatenate([v_all[...].reshape(SEQ * ROWS, HEAD_DIM), ones], axis=1)
        v_text = jnp.concatenate(
            [vt_all[...].reshape(SEQ * TROWS, HEAD_DIM), ones[: SEQ * TROWS]], axis=1
        )
        for i, (image, text) in enumerate(weights):
            summed = jnp.dot(image, v_image, preferred_element_type=F32) + jnp.dot(
                text, v_text, preferred_element_type=F32
            )
            result = (summed[:, :HEAD_DIM] / summed[:, HEAD_DIM:]).astype(BF16)
            att[i * CHUNK : (i + 1) * CHUNK] = result.reshape(CHUNK, ROWS, HEAD_DIM)

        def give(dz, here):
            for dx, xx in zip(FAR_4, xs):
                for dy in reversed(range(QY)):
                    at_y = lax.rem(y + dy, QY)
                    base = lax.rem(z + dz, NZ) * NX + xx
                    slot = base * QY + at_y
                    owner = base * NY + (block * QY + at_y)
                    dst = heads_in.at[cfg, my_head]
                    for copy_index in (other, cfg):
                        if here and dx == 0 and dy == 0 and copy_index is cfg:
                            pltpu.make_async_copy(att.at[slot], dst, recv_sem.at[5]).start()
                        else:
                            device = {"cfg": copy_index, "seq": owner}
                            remote(
                                att.at[slot], dst, send_sem.at[5], recv_sem.at[5], device
                            ).start()

        over_z(give)

    mod_copy.wait_recv()
    wait_bytes(heads_in, recv_sem.at[5])
    parts = heads_in[...].astype(F32)
    average = jnp.sum(jnp.sum(parts, axis=1, keepdims=True), axis=3, keepdims=True) / FEAT
    parts = parts - average
    squares = jnp.sum(parts * parts, axis=1, keepdims=True)
    variance = jnp.sum(squares, axis=3, keepdims=True) / FEAT
    factor = lax.rsqrt(variance + 1e-06)
    normed = (parts * factor * (1.0 + mod[:, 1]) + mod[:, 0]).astype(BF16)
    normed = jnp.concatenate([normed[:, h] for h in range(HEADS)], axis=2)
    velocity = nt_dot(normed.reshape(2 * ROWS, FEAT), w_own[...])
    uncond = velocity[ROWS:]
    guided = uncond + GUIDANCE * (velocity[:ROWS] - uncond)
    position = jnp.broadcast_to(step_ref[...].astype(F32), (1, CHAN))
    delta = sigma_at(position + 1.0) - sigma_at(position)
    latents = lat_own[...] + delta * guided
    square = jnp.sum(
        jnp.sum(latents * latents, axis=1, keepdims=True), axis=0, keepdims=True
    )
    sums[me] = jnp.where(lane == HEADS, square, peak_row[...])

    def share(dz, here):
        base = lax.rem(z + dz, NZ) * (NX * NY)
        for offset in plane[:-1] if here else plane:
            remote(
                sums.at[me],
                sums.at[me],
                send_sem.at[6],
                recv_sem.at[6],
                {"cfg": cfg, "seq": base + offset},
            ).start()

    over_z(share)

    half = CHAN // 2
    out_ref[0, :, :half] = jnp.where(cfg == 0, latents[:, :half], latents[:, half:])
    out_ref[1, :, :half] = jnp.where(cfg == 0, guided[:, :half], guided[:, half:])

    mod_copy.wait_send()

    @pl.when(attends)
    def _():
        wait_bytes(k_all.at[: UNITS - 1], send_sem.at[0])
        wait_bytes(kt_all.at[: UNITS - 1], send_sem.at[1])
        wait_bytes(vt_all.at[: UNITS - 1], send_sem.at[7])
        wait_bytes(q_all.at[: HEADS - 1], send_sem.at[2])
        wait_bytes(v_all.at[: UNITS - 1], send_sem.at[3])
        wait_bytes(k_all.at[: 2 * OWNERS - 1], send_sem.at[5])

    @pl.when(idle)
    def _():
        wait_bytes(k_all.at[:UNITS], send_sem.at[0])
        wait_bytes(kt_all.at[:UNITS], send_sem.at[1])
        wait_bytes(vt_all.at[:UNITS], send_sem.at[7])
        wait_bytes(q_all.at[:HEADS], send_sem.at[2])
        wait_bytes(v_all.at[:UNITS], send_sem.at[3])

    wait_bytes(sums.at[: SEQ - 1], recv_sem.at[6])
    wait_bytes(sums.at[: SEQ - 1], send_sem.at[6])
    rows = sums[...]
    norm = jnp.sqrt(jnp.sum(rows, axis=0) / (SEQ * ROWS * CHAN))
    out_ref[2, 0:1, :] = jnp.where(lane == HEADS, norm, jnp.max(rows, axis=0))


def per_device(
    q_image, k_image, v_image, k_text, v_text, text_len, shift, scale, w_latent, latents, step_index
):
    anywhere = pl.BlockSpec(memory_space=pltpu.HBM)
    vmem = pl.BlockSpec(memory_space=pltpu.VMEM)
    half = CHAN // 2
    packed = pl.pallas_call(
        kernel,
        out_shape=pltpu.VMEM((3, ROWS, HEAD_DIM), F32),
        in_specs=[vmem] * 2 + [anywhere] * 9,
        out_specs=vmem,
        scratch_shapes=[
            pltpu.VMEM((CHAN, FEAT), BF16),
            pltpu.VMEM((ROWS, CHAN), F32),
            pltpu.VMEM((2, 2, HEADS, 1, HEAD_DIM), F32),
            pltpu.VMEM((OWNERS, ROWS, HEAD_DIM), BF16),
            pltpu.VMEM((SEQ, ROWS, HEAD_DIM), BF16),
            pltpu.VMEM((SEQ, TROWS, HEAD_DIM), BF16),
            pltpu.VMEM((SEQ, ROWS, HEAD_DIM), BF16),
            pltpu.VMEM((SEQ, TROWS, HEAD_DIM), BF16),
            pltpu.VMEM((OWNERS, ROWS, HEAD_DIM), BF16),
            pltpu.VMEM((1, HEAD_DIM), F32),
            pltpu.VMEM((2, HEADS, ROWS, HEAD_DIM), BF16),
            pltpu.VMEM((SEQ, 1, HEAD_DIM), F32),
            pltpu.SemaphoreType.DMA((4,)),
            pltpu.SemaphoreType.DMA((8,)),
            pltpu.SemaphoreType.DMA((8,)),
        ],
        compiler_params=pltpu.CompilerParams(collective_id=0, has_side_effects=True),
        name="joint_attention_step",
    )(
        text_len,
        step_index.reshape(1, 1),
        q_image,
        k_image,
        v_image,
        k_text,
        v_text,
        shift.reshape(1, HEADS, 1, HEAD_DIM),
        scale.reshape(1, HEADS, 1, HEAD_DIM),
        w_latent.T,
        latents,
    )
    return (
        packed[0, :, :half],
        packed[1, :, :half],
        packed[2, 0, HEADS : HEADS + 1],
        packed[2, 0:1, :HEADS].reshape(1, 1, HEADS),
    )


def solution(mesh):
    placed = (
        P("cfg", ("req", "seq"), None),
        P("cfg", ("req", "seq"), None),
        P("cfg", ("req", "seq"), None),
        P("cfg", ("req", "seq"), None),
        P("cfg", ("req", "seq"), None),
        P("cfg", "req"),
        P("cfg", "req", None),
        P("cfg", "req", None),
        P(),
        P(("req", "seq"), None),
        P(),
    )
    return jax.shard_map(
        per_device,
        mesh=mesh,
        in_specs=placed,
        out_specs=(
            P(("req", "seq"), "cfg"),
            P(("req", "seq"), "cfg"),
            P("req"),
            P("cfg", "req", None),
        ),
        check_vma=False,
    )
```

```python
import math

import jax
import jax.numpy as jnp
from jax import lax
from jax.experimental import pallas as pl
from jax.experimental.pallas import tpu as pltpu
from jax.sharding import PartitionSpec as P

HEADS = 16
HEAD_DIM = 128
FEAT = HEADS * HEAD_DIM
CHAN = 64
STEPS = 28
GUIDANCE = 3.5
SIGMA_SHIFT = 3.0

NZ, NX, NY = 8, 4, 4
SEQ = NZ * NX * NY
ROWS = 8
TROWS = 4
UZ = HEADS // NX
BLOCKS = 2
QY = NY // BLOCKS
OWNERS = NZ * NX * QY
LZ = 1
LFROM = 1
OPL = NZ // (2 * LZ)
FINAL = 2 * LZ * NX * NY
FINAL_BLOCK = FINAL // BLOCKS
CHUNK = 16
UNITS = HEADS * BLOCKS
FAR_4 = (2, 1, 3, 0)

MESH = pl.DeviceIdType.MESH
BF16 = jnp.bfloat16
F32 = jnp.float32


def remote(src, dst, send_sem, recv_sem, device):
    return pltpu.make_async_remote_copy(
        src_ref=src,
        dst_ref=dst,
        send_sem=send_sem,
        recv_sem=recv_sem,
        device_id=device,
        device_id_type=MESH,
    )


def wait_bytes(ref, sem):
    pltpu.make_async_copy(ref, ref, sem).wait()


def nt_dot(a, b):
    return lax.dot_general(a, b, (((1,), (1,)), ((), ())), preferred_element_type=F32)


def sigma_at(position):
    level = 1.0 - position / STEPS
    return SIGMA_SHIFT * level / (1.0 + (SIGMA_SHIFT - 1.0) * level)


def far_first(i):
    return NZ // 2 + ((i + 1) // 2) * (1 - 2 * lax.rem(i, 2))


def unit_y(z, x, block, cfg):
    return block if QY == 1 else block * QY + lax.rem(z + x + cfg, QY)


def over_z(body):
    def step(i, carry):
        body(far_first(i), False)
        return carry

    lax.fori_loop(0, NZ - 1, step, 0)
    body(0, True)


def kernel(
    len_ref,
    step_ref,
    q_hbm,
    k_hbm,
    v_hbm,
    kt_hbm,
    vt_hbm,
    shift_hbm,
    scale_hbm,
    w_hbm,
    lat_hbm,
    out_ref,
    w_own,
    lat_in,
    mod,
    q_all,
    k_all,
    kt_all,
    v_all,
    vt_all,
    att,
    peak_row,
    heads_in,
    peaks_in,
    result,
    result_in,
    sums,
    local_sem,
    send_sem,
    recv_sem,
):
    cfg = lax.axis_index("cfg")
    me = lax.axis_index("seq")
    other = 1 - cfg
    z = me // (NX * NY)
    x = lax.rem(me // NY, NX)
    y = lax.rem(me, NY)
    block = y // QY
    attends = (z < UZ) & (y == unit_y(z, x, block, cfg))
    idle = jnp.logical_not(attends)
    my_head = z * NX + x
    group = z // OPL
    my_slot = ((group * NX + x) * QY + lax.rem(y, QY)) * OPL + lax.rem(z, OPL)
    finishes = (z >= LFROM) & (z < LFROM + LZ)
    passes = (z < LFROM) | (z >= LFROM + LZ)
    my_group = cfg * LZ + z - LFROM
    my_row = (my_group * NX + x) * NY + y
    gives = cfg == group // LZ
    keeps = gives & (LFROM + lax.rem(group, LZ) == z)
    sends_lat = gives & (LFROM + lax.rem(group, LZ) != z)
    xs = [lax.rem(x + d, NX) for d in FAR_4]
    ys = [lax.rem(y + d, NY) for d in FAR_4]
    plane = [xx * NY + yy for xx in xs for yy in ys]

    loads = [
        (shift_hbm.at[0], mod.at[cfg, 0]),
        (scale_hbm.at[0], mod.at[cfg, 1]),
        (w_hbm, w_own),
    ]
    copies = [pltpu.make_async_copy(s, d, local_sem.at[i]) for i, (s, d) in enumerate(loads)]

    barrier = pltpu.get_barrier_semaphore()

    def greet(device):
        pl.semaphore_signal(barrier, inc=1, device_id=device, device_id_type=MESH)

    greet({"cfg": other, "seq": me})

    @pl.when(attends)
    def _():
        def signals(dz, here):
            base = lax.rem(z + dz, NZ) * (NX * NY)
            for offset in plane[:-1] if here else plane:
                greet({"cfg": cfg, "seq": base + offset})

        over_z(signals)

    @pl.when(finishes)
    def _():
        for j in range(OPL):
            owner_z = my_group * OPL + j

            @pl.when(owner_z != z)
            def _():
                greet({"cfg": cfg, "seq": (owner_z * NX + x) * NY + y})

        for copy in copies:
            copy.start()

    pl.semaphore_wait(
        barrier, UNITS + 1 - jnp.where(attends, 1, 0) + jnp.where(sends_lat, 1, 0)
    )

    def to_units(pieces):
        def sends(zz, here):
            for dx, xx in zip(FAR_4, xs):
                head = zz * NX + xx
                for db in reversed(range(BLOCKS)):
                    unit = head * NY + unit_y(zz, xx, lax.rem(block + db, BLOCKS), cfg)

                    def away():
                        for i, src, dst in pieces(head, db == 0):
                            device = {"cfg": cfg, "seq": unit}
                            remote(src, dst, send_sem.at[i], recv_sem.at[i], device).start()

                    def local():
                        for i, src, dst in pieces(head, True):
                            pltpu.make_async_copy(src, dst, recv_sem.at[i]).start()

                    if here and dx == 0 and db == 0:
                        pl.when(unit != me)(away)
                        pl.when(unit == me)(local)
                    else:
                        away()

        def step(i, carry):
            sends(lax.rem(z + 1 + i, UZ), False)
            return carry

        lax.fori_loop(0, UZ - 1, step, 0)
        sends(lax.rem(z, UZ), True)

    def slice_of(ref, head):
        return ref.at[0, :, pl.ds(pl.multiple_of(head * HEAD_DIM, HEAD_DIM), HEAD_DIM)]

    def keys(head, own_block):
        parts = [
            (0, slice_of(k_hbm, head), k_all.at[me]),
            (1, slice_of(kt_hbm, head), kt_all.at[me]),
        ]
        if own_block:
            parts.append((2, slice_of(q_hbm, head), q_all.at[my_slot]))
        return parts

    def values(head, own_block):
        return [
            (3, slice_of(v_hbm, head), v_all.at[me]),
            (7, slice_of(vt_hbm, head), vt_all.at[me]),
        ]

    to_units(keys)
    to_units(values)

    mod_copy = remote(
        mod.at[cfg], mod.at[cfg], send_sem.at[4], recv_sem.at[4], {"cfg": other, "seq": me}
    )
    taker = ((LFROM + lax.rem(group, LZ)) * NX + x) * NY + y
    lat_slot = lat_in.at[lax.rem(z, OPL)]
    lat_copy = remote(
        lat_hbm, lat_slot, send_sem.at[8], recv_sem.at[8], {"cfg": cfg, "seq": taker}
    )

    @pl.when(sends_lat)
    def _():
        lat_copy.start()

    @pl.when(keeps)
    def _():
        pltpu.make_async_copy(lat_hbm, lat_slot, recv_sem.at[8]).start()

    @pl.when(finishes)
    def _():
        for copy in copies:
            copy.wait()
        mod_copy.start()

    lane = lax.broadcasted_iota(jnp.int32, (1, HEAD_DIM), 1)

    @pl.when(attends)
    def _():
        wait_bytes(k_all, recv_sem.at[0])
        wait_bytes(kt_all, recv_sem.at[1])
        wait_bytes(q_all, recv_sem.at[2])
        inv_root = 1.0 / math.sqrt(HEAD_DIM)
        rate = inv_root * math.log2(math.e)
        keys_image = k_all[...].reshape(SEQ * ROWS, HEAD_DIM)
        keys_text = kt_all[...].reshape(SEQ * TROWS, HEAD_DIM)
        position = lax.broadcasted_iota(jnp.int32, (1, SEQ * TROWS), 1)
        usable = position < len_ref[...]
        weights = []
        top = None
        for start in range(0, OWNERS, CHUNK):
            q = q_all[start : start + CHUNK].reshape(CHUNK * ROWS, HEAD_DIM)
            image = nt_dot(q, keys_image)
            text = jnp.where(usable, nt_dot(q, keys_text), -jnp.inf)
            peak = jnp.maximum(
                jnp.max(image, axis=1, keepdims=True), jnp.max(text, axis=1, keepdims=True)
            )
            image = jnp.exp2((image - peak) * rate).astype(BF16)
            text = jnp.exp2((text - peak) * rate).astype(BF16)
            weights.append((image, text))
            most = jnp.max(peak, axis=0, keepdims=True)
            top = most if top is None else jnp.maximum(top, most)
        peak_row[...] = jnp.where(lane == cfg * HEADS + my_head, top * inv_root, -jnp.inf)
        ones = jnp.ones((SEQ * ROWS, HEAD_DIM), BF16)
        wait_bytes(v_all, recv_sem.at[3])
        wait_bytes(vt_all, recv_sem.at[7])
        v_image = jnp.concatenate([v_all[...].reshape(SEQ * ROWS, HEAD_DIM), ones], axis=1)
        v_text = jnp.concatenate(
            [vt_all[...].reshape(SEQ * TROWS, HEAD_DIM), ones[: SEQ * TROWS]], axis=1
        )
        for i, (image, text) in enumerate(weights):
            summed = jnp.dot(image, v_image, preferred_element_type=F32) + jnp.dot(
                text, v_text, preferred_element_type=F32
            )
            result = (summed[:, :HEAD_DIM] / summed[:, HEAD_DIM:]).astype(BF16)
            att[i * CHUNK : (i + 1) * CHUNK] = result.reshape(CHUNK, ROWS, HEAD_DIM)

        for dx, xx in zip(FAR_4, xs):
            for dy in reversed(range(QY)):
                at_y = lax.rem(y + dy, QY)
                for plane_z in reversed(range(LZ)):
                    target = ((LFROM + plane_z) * NX + xx) * NY + (block * QY + at_y)
                    for copy_index in (other, cfg):
                        k = copy_index * LZ + plane_z
                        first = ((k * NX + xx) * QY + at_y) * OPL
                        moves = [
                            (5, att.at[pl.ds(first, OPL)], heads_in.at[cfg, my_head]),
                            (9, peak_row, peaks_in.at[cfg, my_head]),
                        ]

                        def away():
                            device = {"cfg": copy_index, "seq": target}
                            for i, src, dst in moves:
                                remote(src, dst, send_sem.at[i], recv_sem.at[i], device).start()

                        def local():
                            for i, src, dst in moves:
                                pltpu.make_async_copy(src, dst, recv_sem.at[i]).start()

                        if dx == 0 and dy == 0 and copy_index is cfg:
                            pl.when(LFROM + plane_z != z)(away)
                            pl.when(LFROM + plane_z == z)(local)
                        else:
                            away()

    @pl.when(finishes)
    def _():
        mod_copy.wait_recv()
        wait_bytes(lat_in, recv_sem.at[8])
        wait_bytes(heads_in, recv_sem.at[5])
        wait_bytes(peaks_in, recv_sem.at[9])
        parts = heads_in[...].astype(F32)
        average = jnp.sum(jnp.sum(parts, axis=1, keepdims=True), axis=4, keepdims=True) / FEAT
        parts = parts - average
        squares = jnp.sum(parts * parts, axis=1, keepdims=True)
        variance = jnp.sum(squares, axis=4, keepdims=True) / FEAT
        factor = lax.rsqrt(variance + 1e-06)
        normed = parts * factor * (1.0 + mod[:, 1][:, :, None]) + mod[:, 0][:, :, None]
        normed = normed.reshape(2, HEADS, OPL * ROWS, HEAD_DIM).astype(BF16)
        normed = jnp.concatenate([normed[:, h] for h in range(HEADS)], axis=2)
        velocity = nt_dot(normed.reshape(2 * OPL * ROWS, FEAT), w_own[...])
        uncond = velocity[OPL * ROWS :]
        guided = uncond + GUIDANCE * (velocity[: OPL * ROWS] - uncond)
        position = jnp.broadcast_to(step_ref[...].astype(F32), (1, CHAN))
        delta = sigma_at(position + 1.0) - sigma_at(position)
        latents = lat_in[...].reshape(OPL * ROWS, CHAN) + delta * guided
        square = jnp.sum(
            jnp.sum(latents * latents, axis=1, keepdims=True), axis=0, keepdims=True
        )
        tops = jnp.max(peaks_in[...].reshape(2 * HEADS, 1, HEAD_DIM), axis=0)
        sums[my_row] = jnp.where(lane == 2 * HEADS, square, tops)
        done = jnp.concatenate([latents, guided], axis=1)
        result[:OPL] = done.reshape(OPL, ROWS, HEAD_DIM)

        def share(base, skip):
            for offset in plane:
                for copy_index in (cfg, other):
                    if skip and offset is plane[-1] and copy_index is cfg:
                        continue
                    remote(
                        sums.at[my_row],
                        sums.at[my_row],
                        send_sem.at[6],
                        recv_sem.at[6],
                        {"cfg": copy_index, "seq": base + offset},
                    ).start()

        share(lax.rem(z + NZ - 1, NZ) * (NX * NY), False)
        share(z * (NX * NY), True)
        for j in range(OPL):
            owner_z = my_group * OPL + j
            for copy_index in (cfg, other):

                def away():
                    device = {"cfg": copy_index, "seq": (owner_z * NX + x) * NY + y}
                    remote(
                        result.at[j], result_in, send_sem.at[10], recv_sem.at[10], device
                    ).start()

                def local():
                    pltpu.make_async_copy(result.at[j], result_in, recv_sem.at[10]).start()

                if copy_index is cfg:
                    pl.when(owner_z != z)(away)
                    pl.when(owner_z == z)(local)
                else:
                    away()

        def step(i, carry):
            share(lax.rem(z + 1 + i, NZ) * (NX * NY), False)
            return carry

        lax.fori_loop(0, NZ - 2, step, 0)

    wait_bytes(result_in, recv_sem.at[10])
    latents = result_in[:, :CHAN]
    guided = result_in[:, CHAN:]
    half = CHAN // 2
    out_ref[0, :, :half] = jnp.where(cfg == 0, latents[:, :half], latents[:, half:])
    out_ref[1, :, :half] = jnp.where(cfg == 0, guided[:, :half], guided[:, half:])

    @pl.when(sends_lat)
    def _():
        lat_copy.wait_send()

    @pl.when(attends)
    def _():
        wait_bytes(k_all.at[: UNITS - 1], send_sem.at[0])
        wait_bytes(kt_all.at[: UNITS - 1], send_sem.at[1])
        wait_bytes(q_all.at[: HEADS - 1], send_sem.at[2])
        wait_bytes(v_all.at[: UNITS - 1], send_sem.at[3])
        wait_bytes(vt_all.at[: UNITS - 1], send_sem.at[7])

    @pl.when(idle)
    def _():
        wait_bytes(k_all.at[:UNITS], send_sem.at[0])
        wait_bytes(kt_all.at[:UNITS], send_sem.at[1])
        wait_bytes(q_all.at[:HEADS], send_sem.at[2])
        wait_bytes(v_all.at[:UNITS], send_sem.at[3])
        wait_bytes(vt_all.at[:UNITS], send_sem.at[7])

    @pl.when(attends & finishes)
    def _():
        wait_bytes(att.at[: OWNERS - OPL], send_sem.at[5])
        wait_bytes(sums.at[: FINAL_BLOCK - 1], send_sem.at[9])

    @pl.when(attends & passes)
    def _():
        wait_bytes(att, send_sem.at[5])
        wait_bytes(sums.at[:FINAL_BLOCK], send_sem.at[9])

    @pl.when(finishes)
    def _():
        mod_copy.wait_send()
        wait_bytes(sums.at[: FINAL - 1], recv_sem.at[6])

    @pl.when(passes)
    def _():
        wait_bytes(sums.at[:FINAL], recv_sem.at[6])

    rows = sums[:FINAL]
    norm = jnp.sqrt(jnp.sum(rows, axis=0) / (SEQ * ROWS * CHAN))
    tops = jnp.max(rows, axis=0)
    out_ref[2, 0:1, :HEADS] = jnp.where(cfg == 0, tops[:, :HEADS], tops[:, HEADS : 2 * HEADS])
    out_ref[2, 1:2, :] = norm

    @pl.when(finishes)
    def _():
        wait_bytes(sums.at[: 2 * SEQ - 1], send_sem.at[6])

    @pl.when(finishes & keeps)
    def _():
        wait_bytes(result.at[: 2 * OPL - 1], send_sem.at[10])

    @pl.when(finishes & jnp.logical_not(keeps))
    def _():
        wait_bytes(result, send_sem.at[10])


def per_device(
    q_image, k_image, v_image, k_text, v_text, text_len, shift, scale, w_latent, latents, step_index
):
    anywhere = pl.BlockSpec(memory_space=pltpu.HBM)
    vmem = pl.BlockSpec(memory_space=pltpu.VMEM)
    half = CHAN // 2
    packed = pl.pallas_call(
        kernel,
        out_shape=pltpu.VMEM((3, ROWS, HEAD_DIM), F32),
        in_specs=[vmem] * 2 + [anywhere] * 9,
        out_specs=vmem,
        scratch_shapes=[
            pltpu.VMEM((CHAN, FEAT), BF16),
            pltpu.VMEM((OPL, ROWS, CHAN), F32),
            pltpu.VMEM((2, 2, HEADS, 1, HEAD_DIM), F32),
            pltpu.VMEM((OWNERS, ROWS, HEAD_DIM), BF16),
            pltpu.VMEM((SEQ, ROWS, HEAD_DIM), BF16),
            pltpu.VMEM((SEQ, TROWS, HEAD_DIM), BF16),
            pltpu.VMEM((SEQ, ROWS, HEAD_DIM), BF16),
            pltpu.VMEM((SEQ, TROWS, HEAD_DIM), BF16),
            pltpu.VMEM((OWNERS, ROWS, HEAD_DIM), BF16),
            pltpu.VMEM((1, HEAD_DIM), F32),
            pltpu.VMEM((2, HEADS, OPL, ROWS, HEAD_DIM), BF16),
            pltpu.VMEM((2, HEADS, 1, HEAD_DIM), F32),
            pltpu.VMEM((2 * OPL, ROWS, HEAD_DIM), F32),
            pltpu.VMEM((ROWS, HEAD_DIM), F32),
            pltpu.VMEM((2 * SEQ, 1, HEAD_DIM), F32),
            pltpu.SemaphoreType.DMA((3,)),
            pltpu.SemaphoreType.DMA((11,)),
            pltpu.SemaphoreType.DMA((11,)),
        ],
        compiler_params=pltpu.CompilerParams(collective_id=0, has_side_effects=True),
        name="joint_attention_step",
    )(
        text_len,
        step_index.reshape(1, 1),
        q_image,
        k_image,
        v_image,
        k_text,
        v_text,
        shift.reshape(1, HEADS, 1, HEAD_DIM),
        scale.reshape(1, HEADS, 1, HEAD_DIM),
        w_latent.T,
        latents,
    )
    return (
        packed[0, :, :half],
        packed[1, :, :half],
        packed[2, 1, 2 * HEADS : 2 * HEADS + 1],
        packed[2, 0:1, :HEADS].reshape(1, 1, HEADS),
    )


def solution(mesh):
    placed = (
        P("cfg", ("req", "seq"), None),
        P("cfg", ("req", "seq"), None),
        P("cfg", ("req", "seq"), None),
        P("cfg", ("req", "seq"), None),
        P("cfg", ("req", "seq"), None),
        P("cfg", "req"),
        P("cfg", "req", None),
        P("cfg", "req", None),
        P(),
        P(("req", "seq"), None),
        P(),
    )
    return jax.shard_map(
        per_device,
        mesh=mesh,
        in_specs=placed,
        out_specs=(
            P(("req", "seq"), "cfg"),
            P(("req", "seq"), "cfg"),
            P("req"),
            P("cfg", "req", None),
        ),
        check_vma=False,
    )
```

```python
import math

import jax
import jax.numpy as jnp
from jax import lax
from jax.experimental import pallas as pl
from jax.experimental.pallas import tpu as pltpu
from jax.sharding import PartitionSpec as P

HEADS = 16
HEAD_DIM = 128
FEAT = HEADS * HEAD_DIM
CHAN = 64
STEPS = 28
GUIDANCE = 3.5
SIGMA_SHIFT = 3.0

NZ, NX, NY = 8, 4, 4
SEQ = NZ * NX * NY
ROWS = 8
TROWS = 4
UZ = HEADS // NX
BLOCKS = 2
QY = NY // BLOCKS
OWNERS = NZ * NX * QY
LZ = 1
LFROM = 1
OPL = NZ // (2 * LZ)
FINAL = 2 * LZ * NX * NY
FINAL_BLOCK = FINAL // BLOCKS
CHUNK = 16
UNITS = HEADS * BLOCKS
FAR_4 = (2, 1, 3, 0)

MESH = pl.DeviceIdType.MESH
BF16 = jnp.bfloat16
F32 = jnp.float32


def remote(src, dst, send_sem, recv_sem, device):
    return pltpu.make_async_remote_copy(
        src_ref=src,
        dst_ref=dst,
        send_sem=send_sem,
        recv_sem=recv_sem,
        device_id=device,
        device_id_type=MESH,
    )


def wait_bytes(ref, sem):
    pltpu.make_async_copy(ref, ref, sem).wait()


def nt_dot(a, b):
    return lax.dot_general(a, b, (((1,), (1,)), ((), ())), preferred_element_type=F32)


def sigma_at(position):
    level = 1.0 - position / STEPS
    return SIGMA_SHIFT * level / (1.0 + (SIGMA_SHIFT - 1.0) * level)


def far_first(i):
    return NZ // 2 + ((i + 1) // 2) * (1 - 2 * lax.rem(i, 2))


def unit_y(z, x, block, cfg):
    return block if QY == 1 else block * QY + lax.rem(z + x + cfg, QY)


def over_z(body):
    def step(i, carry):
        body(far_first(i), False)
        return carry

    lax.fori_loop(0, NZ - 1, step, 0)
    body(0, True)


def kernel(
    len_ref,
    step_ref,
    q_hbm,
    k_hbm,
    v_hbm,
    kt_hbm,
    vt_hbm,
    shift_hbm,
    scale_hbm,
    w_hbm,
    lat_hbm,
    out_ref,
    q_own,
    k_own,
    v_own,
    kt_own,
    vt_own,
    w_own,
    lat_in,
    mod,
    q_all,
    k_all,
    kt_all,
    v_all,
    vt_all,
    att,
    peak_row,
    heads_in,
    peaks_in,
    result,
    result_in,
    sums,
    local_sem,
    send_sem,
    recv_sem,
):
    cfg = lax.axis_index("cfg")
    me = lax.axis_index("seq")
    other = 1 - cfg
    z = me // (NX * NY)
    x = lax.rem(me // NY, NX)
    y = lax.rem(me, NY)
    block = y // QY
    attends = (z < UZ) & (y == unit_y(z, x, block, cfg))
    idle = jnp.logical_not(attends)
    my_head = z * NX + x
    group = z // OPL
    my_slot = ((group * NX + x) * QY + lax.rem(y, QY)) * OPL + lax.rem(z, OPL)
    finishes = (z >= LFROM) & (z < LFROM + LZ)
    passes = (z < LFROM) | (z >= LFROM + LZ)
    my_group = cfg * LZ + z - LFROM
    my_row = (my_group * NX + x) * NY + y
    gives = cfg == group // LZ
    keeps = gives & (LFROM + lax.rem(group, LZ) == z)
    sends_lat = gives & (LFROM + lax.rem(group, LZ) != z)
    xs = [lax.rem(x + d, NX) for d in FAR_4]
    ys = [lax.rem(y + d, NY) for d in FAR_4]
    plane = [xx * NY + yy for xx in xs for yy in ys]

    sources = [
        (k_hbm, k_own),
        (kt_hbm, kt_own),
        (q_hbm, q_own),
        (v_hbm, v_own),
        (vt_hbm, vt_own),
    ]
    staged = [
        pltpu.make_async_copy(s.at[0], d, local_sem.at[3 + i]) for i, (s, d) in enumerate(sources)
    ]
    for copy in staged:
        copy.start()
    loads = [
        (shift_hbm.at[0], mod.at[cfg, 0]),
        (scale_hbm.at[0], mod.at[cfg, 1]),
        (w_hbm, w_own),
    ]
    copies = [pltpu.make_async_copy(s, d, local_sem.at[i]) for i, (s, d) in enumerate(loads)]

    barrier = pltpu.get_barrier_semaphore()

    def greet(device):
        pl.semaphore_signal(barrier, inc=1, device_id=device, device_id_type=MESH)

    greet({"cfg": other, "seq": me})

    @pl.when(attends)
    def _():
        def signals(dz, here):
            base = lax.rem(z + dz, NZ) * (NX * NY)
            for offset in plane[:-1] if here else plane:
                greet({"cfg": cfg, "seq": base + offset})

        over_z(signals)

    @pl.when(finishes)
    def _():
        for j in range(OPL):
            owner_z = my_group * OPL + j

            @pl.when(owner_z != z)
            def _():
                greet({"cfg": cfg, "seq": (owner_z * NX + x) * NY + y})

        for copy in copies:
            copy.start()

    pl.semaphore_wait(
        barrier, UNITS + 1 - jnp.where(attends, 1, 0) + jnp.where(sends_lat, 1, 0)
    )

    for copy in staged:
        copy.wait()

    def to_units(pieces):
        def sends(zz, here):
            for dx, xx in zip(FAR_4, xs):
                head = zz * NX + xx
                for db in reversed(range(BLOCKS)):
                    unit = head * NY + unit_y(zz, xx, lax.rem(block + db, BLOCKS), cfg)

                    def away():
                        for i, src, dst in pieces(head, db == 0):
                            device = {"cfg": cfg, "seq": unit}
                            remote(src, dst, send_sem.at[i], recv_sem.at[i], device).start()

                    def local():
                        for i, src, dst in pieces(head, True):
                            pltpu.make_async_copy(src, dst, recv_sem.at[i]).start()

                    if here and dx == 0 and db == 0:
                        pl.when(unit != me)(away)
                        pl.when(unit == me)(local)
                    else:
                        away()

        near = jnp.where(z < UZ, z + 1, z)

        def step(i, carry):
            sends(lax.rem(near + i, UZ), False)
            return carry

        lax.fori_loop(0, UZ - 1, step, 0)
        sends(lax.rem(near + UZ - 1, UZ), True)

    def slice_of(ref, head):
        return ref.at[:, pl.ds(pl.multiple_of(head * HEAD_DIM, HEAD_DIM), HEAD_DIM)]

    def keys(head, own_block):
        parts = [
            (0, slice_of(k_own, head), k_all.at[me]),
            (1, slice_of(kt_own, head), kt_all.at[me]),
        ]
        if own_block:
            parts.append((2, slice_of(q_own, head), q_all.at[my_slot]))
        return parts

    def values(head, own_block):
        return [
            (3, slice_of(v_own, head), v_all.at[me]),
            (7, slice_of(vt_own, head), vt_all.at[me]),
        ]

    to_units(keys)
    to_units(values)

    mod_copy = remote(
        mod.at[cfg], mod.at[cfg], send_sem.at[4], recv_sem.at[4], {"cfg": other, "seq": me}
    )
    taker = ((LFROM + lax.rem(group, LZ)) * NX + x) * NY + y
    lat_slot = lat_in.at[lax.rem(z, OPL)]
    lat_copy = remote(
        lat_hbm, lat_slot, send_sem.at[8], recv_sem.at[8], {"cfg": cfg, "seq": taker}
    )

    @pl.when(sends_lat)
    def _():
        lat_copy.start()

    @pl.when(keeps)
    def _():
        pltpu.make_async_copy(lat_hbm, lat_slot, recv_sem.at[8]).start()

    @pl.when(finishes)
    def _():
        for copy in copies:
            copy.wait()
        mod_copy.start()

    lane = lax.broadcasted_iota(jnp.int32, (1, HEAD_DIM), 1)

    @pl.when(attends)
    def _():
        wait_bytes(k_all, recv_sem.at[0])
        wait_bytes(kt_all, recv_sem.at[1])
        wait_bytes(q_all, recv_sem.at[2])
        inv_root = 1.0 / math.sqrt(HEAD_DIM)
        rate = inv_root * math.log2(math.e)
        keys_image = k_all[...].reshape(SEQ * ROWS, HEAD_DIM)
        keys_text = kt_all[...].reshape(SEQ * TROWS, HEAD_DIM)
        position = lax.broadcasted_iota(jnp.int32, (1, SEQ * TROWS), 1)
        usable = position < len_ref[...]
        weights = []
        top = None
        for start in range(0, OWNERS, CHUNK):
            q = q_all[start : start + CHUNK].reshape(CHUNK * ROWS, HEAD_DIM)
            image = nt_dot(q, keys_image)
            text = jnp.where(usable, nt_dot(q, keys_text), -jnp.inf)
            peak = jnp.maximum(
                jnp.max(image, axis=1, keepdims=True), jnp.max(text, axis=1, keepdims=True)
            )
            image = jnp.exp2((image - peak) * rate).astype(BF16)
            text = jnp.exp2((text - peak) * rate).astype(BF16)
            weights.append((image, text))
            most = jnp.max(peak, axis=0, keepdims=True)
            top = most if top is None else jnp.maximum(top, most)
        peak_row[...] = jnp.where(lane == cfg * HEADS + my_head, top * inv_root, -jnp.inf)
        ones = jnp.ones((SEQ * ROWS, HEAD_DIM), BF16)
        wait_bytes(v_all, recv_sem.at[3])
        wait_bytes(vt_all, recv_sem.at[7])
        v_image = jnp.concatenate([v_all[...].reshape(SEQ * ROWS, HEAD_DIM), ones], axis=1)
        v_text = jnp.concatenate(
            [vt_all[...].reshape(SEQ * TROWS, HEAD_DIM), ones[: SEQ * TROWS]], axis=1
        )
        for i, (image, text) in enumerate(weights):
            summed = jnp.dot(image, v_image, preferred_element_type=F32) + jnp.dot(
                text, v_text, preferred_element_type=F32
            )
            result = (summed[:, :HEAD_DIM] / summed[:, HEAD_DIM:]).astype(BF16)
            att[i * CHUNK : (i + 1) * CHUNK] = result.reshape(CHUNK, ROWS, HEAD_DIM)

        for dx, xx in zip(FAR_4, xs):
            for dy in reversed(range(QY)):
                at_y = lax.rem(y + dy, QY)
                for plane_z in reversed(range(LZ)):
                    target = ((LFROM + plane_z) * NX + xx) * NY + (block * QY + at_y)
                    for copy_index in (other, cfg):
                        k = copy_index * LZ + plane_z
                        first = ((k * NX + xx) * QY + at_y) * OPL
                        moves = [
                            (5, att.at[pl.ds(first, OPL)], heads_in.at[cfg, my_head]),
                            (9, peak_row, peaks_in.at[cfg, my_head]),
                        ]

                        def away():
                            device = {"cfg": copy_index, "seq": target}
                            for i, src, dst in moves:
                                remote(src, dst, send_sem.at[i], recv_sem.at[i], device).start()

                        def local():
                            for i, src, dst in moves:
                                pltpu.make_async_copy(src, dst, recv_sem.at[i]).start()

                        if dx == 0 and dy == 0 and copy_index is cfg:
                            pl.when(LFROM + plane_z != z)(away)
                            pl.when(LFROM + plane_z == z)(local)
                        else:
                            away()

    @pl.when(finishes)
    def _():
        mod_copy.wait_recv()
        wait_bytes(lat_in, recv_sem.at[8])
        wait_bytes(heads_in, recv_sem.at[5])
        wait_bytes(peaks_in, recv_sem.at[9])
        parts = heads_in[...].astype(F32)
        average = jnp.sum(jnp.sum(parts, axis=1, keepdims=True), axis=4, keepdims=True) / FEAT
        parts = parts - average
        squares = jnp.sum(parts * parts, axis=1, keepdims=True)
        variance = jnp.sum(squares, axis=4, keepdims=True) / FEAT
        factor = lax.rsqrt(variance + 1e-06)
        normed = parts * factor * (1.0 + mod[:, 1][:, :, None]) + mod[:, 0][:, :, None]
        normed = normed.reshape(2, HEADS, OPL * ROWS, HEAD_DIM).astype(BF16)
        normed = jnp.concatenate([normed[:, h] for h in range(HEADS)], axis=2)
        velocity = nt_dot(normed.reshape(2 * OPL * ROWS, FEAT), w_own[...])
        uncond = velocity[OPL * ROWS :]
        guided = uncond + GUIDANCE * (velocity[: OPL * ROWS] - uncond)
        position = jnp.broadcast_to(step_ref[...].astype(F32), (1, CHAN))
        delta = sigma_at(position + 1.0) - sigma_at(position)
        latents = lat_in[...].reshape(OPL * ROWS, CHAN) + delta * guided
        square = jnp.sum(
            jnp.sum(latents * latents, axis=1, keepdims=True), axis=0, keepdims=True
        )
        tops = jnp.max(peaks_in[...].reshape(2 * HEADS, 1, HEAD_DIM), axis=0)
        sums[my_row] = jnp.where(lane == 2 * HEADS, square, tops)
        done = jnp.concatenate([latents, guided], axis=1)
        result[:OPL] = done.reshape(OPL, ROWS, HEAD_DIM)

        def share(base, skip):
            for offset in plane:
                for copy_index in (cfg, other):
                    if skip and offset is plane[-1] and copy_index is cfg:
                        continue
                    remote(
                        sums.at[my_row],
                        sums.at[my_row],
                        send_sem.at[6],
                        recv_sem.at[6],
                        {"cfg": copy_index, "seq": base + offset},
                    ).start()

        share(lax.rem(z + NZ - 1, NZ) * (NX * NY), False)
        share(z * (NX * NY), True)
        for j in range(OPL):
            owner_z = my_group * OPL + j
            for copy_index in (cfg, other):

                def away():
                    device = {"cfg": copy_index, "seq": (owner_z * NX + x) * NY + y}
                    remote(
                        result.at[j], result_in, send_sem.at[10], recv_sem.at[10], device
                    ).start()

                def local():
                    pltpu.make_async_copy(result.at[j], result_in, recv_sem.at[10]).start()

                if copy_index is cfg:
                    pl.when(owner_z != z)(away)
                    pl.when(owner_z == z)(local)
                else:
                    away()

        def step(i, carry):
            share(lax.rem(z + 1 + i, NZ) * (NX * NY), False)
            return carry

        lax.fori_loop(0, NZ - 2, step, 0)

    wait_bytes(result_in, recv_sem.at[10])
    latents = result_in[:, :CHAN]
    guided = result_in[:, CHAN:]
    half = CHAN // 2
    out_ref[0, :, :half] = jnp.where(cfg == 0, latents[:, :half], latents[:, half:])
    out_ref[1, :, :half] = jnp.where(cfg == 0, guided[:, :half], guided[:, half:])

    @pl.when(sends_lat)
    def _():
        lat_copy.wait_send()

    @pl.when(attends)
    def _():
        wait_bytes(k_all.at[: UNITS - 1], send_sem.at[0])
        wait_bytes(kt_all.at[: UNITS - 1], send_sem.at[1])
        wait_bytes(q_all.at[: HEADS - 1], send_sem.at[2])
        wait_bytes(v_all.at[: UNITS - 1], send_sem.at[3])
        wait_bytes(vt_all.at[: UNITS - 1], send_sem.at[7])

    @pl.when(idle)
    def _():
        wait_bytes(k_all.at[:UNITS], send_sem.at[0])
        wait_bytes(kt_all.at[:UNITS], send_sem.at[1])
        wait_bytes(q_all.at[:HEADS], send_sem.at[2])
        wait_bytes(v_all.at[:UNITS], send_sem.at[3])
        wait_bytes(vt_all.at[:UNITS], send_sem.at[7])

    @pl.when(attends & finishes)
    def _():
        wait_bytes(att.at[: OWNERS - OPL], send_sem.at[5])
        wait_bytes(sums.at[: FINAL_BLOCK - 1], send_sem.at[9])

    @pl.when(attends & passes)
    def _():
        wait_bytes(att, send_sem.at[5])
        wait_bytes(sums.at[:FINAL_BLOCK], send_sem.at[9])

    @pl.when(finishes)
    def _():
        mod_copy.wait_send()
        wait_bytes(sums.at[: FINAL - 1], recv_sem.at[6])

    @pl.when(passes)
    def _():
        wait_bytes(sums.at[:FINAL], recv_sem.at[6])

    rows = sums[:FINAL]
    norm = jnp.sqrt(jnp.sum(rows, axis=0) / (SEQ * ROWS * CHAN))
    tops = jnp.max(rows, axis=0)
    out_ref[2, 0:1, :HEADS] = jnp.where(cfg == 0, tops[:, :HEADS], tops[:, HEADS : 2 * HEADS])
    out_ref[2, 1:2, :] = norm

    @pl.when(finishes)
    def _():
        wait_bytes(sums.at[: 2 * SEQ - 1], send_sem.at[6])

    @pl.when(finishes & keeps)
    def _():
        wait_bytes(result.at[: 2 * OPL - 1], send_sem.at[10])

    @pl.when(finishes & jnp.logical_not(keeps))
    def _():
        wait_bytes(result, send_sem.at[10])


def per_device(
    q_image, k_image, v_image, k_text, v_text, text_len, shift, scale, w_latent, latents, step_index
):
    anywhere = pl.BlockSpec(memory_space=pltpu.HBM)
    vmem = pl.BlockSpec(memory_space=pltpu.VMEM)
    half = CHAN // 2
    packed = pl.pallas_call(
        kernel,
        out_shape=pltpu.VMEM((3, ROWS, HEAD_DIM), F32),
        in_specs=[vmem] * 2 + [anywhere] * 9,
        out_specs=vmem,
        scratch_shapes=[
            pltpu.VMEM((ROWS, FEAT), BF16),
            pltpu.VMEM((ROWS, FEAT), BF16),
            pltpu.VMEM((ROWS, FEAT), BF16),
            pltpu.VMEM((TROWS, FEAT), BF16),
            pltpu.VMEM((TROWS, FEAT), BF16),
            pltpu.VMEM((CHAN, FEAT), BF16),
            pltpu.VMEM((OPL, ROWS, CHAN), F32),
            pltpu.VMEM((2, 2, HEADS, 1, HEAD_DIM), F32),
            pltpu.VMEM((OWNERS, ROWS, HEAD_DIM), BF16),
            pltpu.VMEM((SEQ, ROWS, HEAD_DIM), BF16),
            pltpu.VMEM((SEQ, TROWS, HEAD_DIM), BF16),
            pltpu.VMEM((SEQ, ROWS, HEAD_DIM), BF16),
            pltpu.VMEM((SEQ, TROWS, HEAD_DIM), BF16),
            pltpu.VMEM((OWNERS, ROWS, HEAD_DIM), BF16),
            pltpu.VMEM((1, HEAD_DIM), F32),
            pltpu.VMEM((2, HEADS, OPL, ROWS, HEAD_DIM), BF16),
            pltpu.VMEM((2, HEADS, 1, HEAD_DIM), F32),
            pltpu.VMEM((2 * OPL, ROWS, HEAD_DIM), F32),
            pltpu.VMEM((ROWS, HEAD_DIM), F32),
            pltpu.VMEM((2 * SEQ, 1, HEAD_DIM), F32),
            pltpu.SemaphoreType.DMA((8,)),
            pltpu.SemaphoreType.DMA((11,)),
            pltpu.SemaphoreType.DMA((11,)),
        ],
        compiler_params=pltpu.CompilerParams(collective_id=0, has_side_effects=True),
        name="joint_attention_step",
    )(
        text_len,
        step_index.reshape(1, 1),
        q_image,
        k_image,
        v_image,
        k_text,
        v_text,
        shift.reshape(1, HEADS, 1, HEAD_DIM),
        scale.reshape(1, HEADS, 1, HEAD_DIM),
        w_latent.T,
        latents,
    )
    return (
        packed[0, :, :half],
        packed[1, :, :half],
        packed[2, 1, 2 * HEADS : 2 * HEADS + 1],
        packed[2, 0:1, :HEADS].reshape(1, 1, HEADS),
    )


def solution(mesh):
    placed = (
        P("cfg", ("req", "seq"), None),
        P("cfg", ("req", "seq"), None),
        P("cfg", ("req", "seq"), None),
        P("cfg", ("req", "seq"), None),
        P("cfg", ("req", "seq"), None),
        P("cfg", "req"),
        P("cfg", "req", None),
        P("cfg", "req", None),
        P(),
        P(("req", "seq"), None),
        P(),
    )
    return jax.shard_map(
        per_device,
        mesh=mesh,
        in_specs=placed,
        out_specs=(
            P(("req", "seq"), "cfg"),
            P(("req", "seq"), "cfg"),
            P("req"),
            P("cfg", "req", None),
        ),
        check_vma=False,
    )
```

```python
import math

import jax
import jax.numpy as jnp
from jax import lax
from jax.experimental import pallas as pl
from jax.experimental.pallas import tpu as pltpu
from jax.sharding import PartitionSpec as P

HEADS = 16
HEAD_DIM = 128
FEAT = HEADS * HEAD_DIM
CHAN = 64
STEPS = 28
GUIDANCE = 3.5
SIGMA_SHIFT = 3.0

NZ, NX, NY = 8, 4, 4
SEQ = NZ * NX * NY
ROWS = 8
TROWS = 4
UZ = HEADS // NX
BLOCKS = 2
QY = NY // BLOCKS
OWNERS = NZ * NX * QY
LZ = 1
LFROM = 1
OPL = NZ // (2 * LZ)
FINAL = 2 * LZ * NX * NY
FINAL_BLOCK = FINAL // BLOCKS
CHUNK = 16
UNITS = HEADS * BLOCKS
FAR_4 = (2, 1, 3, 0)

MESH = pl.DeviceIdType.MESH
BF16 = jnp.bfloat16
F32 = jnp.float32


def remote(src, dst, send_sem, recv_sem, device):
    return pltpu.make_async_remote_copy(
        src_ref=src,
        dst_ref=dst,
        send_sem=send_sem,
        recv_sem=recv_sem,
        device_id=device,
        device_id_type=MESH,
    )


def wait_bytes(ref, sem):
    pltpu.make_async_copy(ref, ref, sem).wait()


def nt_dot(a, b):
    return lax.dot_general(a, b, (((1,), (1,)), ((), ())), preferred_element_type=F32)


def sigma_at(position):
    level = 1.0 - position / STEPS
    return SIGMA_SHIFT * level / (1.0 + (SIGMA_SHIFT - 1.0) * level)


def far_first(i):
    return NZ // 2 + ((i + 1) // 2) * (1 - 2 * lax.rem(i, 2))


def unit_y(z, x, block, cfg):
    return block if QY == 1 else block * QY + lax.rem(z + x + cfg, QY)


def over_z(body):
    def step(i, carry):
        body(far_first(i), False)
        return carry

    lax.fori_loop(0, NZ - 1, step, 0)
    body(0, True)


def kernel(
    len_ref,
    step_ref,
    q_hbm,
    k_hbm,
    v_hbm,
    kt_hbm,
    vt_hbm,
    shift_hbm,
    scale_hbm,
    w_hbm,
    lat_hbm,
    out_ref,
    q_own,
    k_own,
    v_own,
    kt_own,
    vt_own,
    w_own,
    lat_in,
    mod,
    q_all,
    k_all,
    kt_all,
    v_all,
    vt_all,
    att,
    peak_row,
    heads_in,
    peaks_in,
    result,
    result_in,
    sums,
    local_sem,
    send_sem,
    recv_sem,
):
    cfg = lax.axis_index("cfg")
    me = lax.axis_index("seq")
    other = 1 - cfg
    z = me // (NX * NY)
    x = lax.rem(me // NY, NX)
    y = lax.rem(me, NY)
    block = y // QY
    attends = (z < UZ) & (y == unit_y(z, x, block, cfg))
    idle = jnp.logical_not(attends)
    my_head = z * NX + x
    group = z // OPL
    my_slot = ((group * NX + x) * QY + lax.rem(y, QY)) * OPL + lax.rem(z, OPL)
    finishes = (z >= LFROM) & (z < LFROM + LZ)
    passes = (z < LFROM) | (z >= LFROM + LZ)
    my_group = cfg * LZ + z - LFROM
    my_row = (my_group * NX + x) * NY + y
    gives = cfg == group // LZ
    keeps = gives & (LFROM + lax.rem(group, LZ) == z)
    sends_lat = gives & (LFROM + lax.rem(group, LZ) != z)
    xs = [lax.rem(x + d, NX) for d in FAR_4]
    ys = [lax.rem(y + d, NY) for d in FAR_4]
    plane = [xx * NY + yy for xx in xs for yy in ys]

    sources = [
        (k_hbm, k_own),
        (kt_hbm, kt_own),
        (q_hbm, q_own),
        (v_hbm, v_own),
        (vt_hbm, vt_own),
    ]
    staged = [
        pltpu.make_async_copy(s.at[0], d, local_sem.at[3 + i]) for i, (s, d) in enumerate(sources)
    ]
    loads = [
        (shift_hbm.at[0], mod.at[cfg, 0]),
        (scale_hbm.at[0], mod.at[cfg, 1]),
        (w_hbm, w_own),
    ]
    copies = [pltpu.make_async_copy(s, d, local_sem.at[i]) for i, (s, d) in enumerate(loads)]

    barrier = pltpu.get_barrier_semaphore()

    def greet(device):
        pl.semaphore_signal(barrier, inc=1, device_id=device, device_id_type=MESH)

    greet({"cfg": other, "seq": me})

    @pl.when(attends)
    def _():
        def signals(dz, here):
            base = lax.rem(z + dz, NZ) * (NX * NY)
            for offset in plane[:-1] if here else plane:
                greet({"cfg": cfg, "seq": base + offset})

        for dz in (4, 3, 5, 2, 6, 1, 7):
            signals(dz, False)
        signals(0, True)

    for copy in staged:
        copy.start()

    @pl.when(finishes)
    def _():
        for j in range(OPL):
            owner_z = my_group * OPL + j

            @pl.when(owner_z != z)
            def _():
                greet({"cfg": cfg, "seq": (owner_z * NX + x) * NY + y})

        for copy in copies:
            copy.start()

    pl.semaphore_wait(
        barrier, UNITS + 1 - jnp.where(attends, 1, 0) + jnp.where(sends_lat, 1, 0)
    )

    for copy in staged:
        copy.wait()

    def to_units(pieces):
        def sends(zz, here):
            for dx, xx in zip(FAR_4, xs):
                head = zz * NX + xx
                for db in reversed(range(BLOCKS)):
                    unit = head * NY + unit_y(zz, xx, lax.rem(block + db, BLOCKS), cfg)

                    def away():
                        for i, src, dst in pieces(head, db == 0):
                            device = {"cfg": cfg, "seq": unit}
                            remote(src, dst, send_sem.at[i], recv_sem.at[i], device).start()

                    def local():
                        for i, src, dst in pieces(head, True):
                            pltpu.make_async_copy(src, dst, recv_sem.at[i]).start()

                    if here and dx == 0 and db == 0:
                        pl.when(unit != me)(away)
                        pl.when(unit == me)(local)
                    else:
                        away()

        near = jnp.where(z < UZ, z + 1, z)

        def step(i, carry):
            sends(lax.rem(near + i, UZ), False)
            return carry

        lax.fori_loop(0, UZ - 1, step, 0)
        sends(lax.rem(near + UZ - 1, UZ), True)

    def slice_of(ref, head):
        return ref.at[:, pl.ds(pl.multiple_of(head * HEAD_DIM, HEAD_DIM), HEAD_DIM)]

    def keys(head, own_block):
        parts = [
            (0, slice_of(k_own, head), k_all.at[me]),
            (1, slice_of(kt_own, head), kt_all.at[me]),
        ]
        if own_block:
            parts.append((2, slice_of(q_own, head), q_all.at[my_slot]))
        return parts

    def values(head, own_block):
        return [
            (3, slice_of(v_own, head), v_all.at[me]),
            (7, slice_of(vt_own, head), vt_all.at[me]),
        ]

    to_units(keys)
    to_units(values)

    mod_copy = remote(
        mod.at[cfg], mod.at[cfg], send_sem.at[4], recv_sem.at[4], {"cfg": other, "seq": me}
    )
    taker = ((LFROM + lax.rem(group, LZ)) * NX + x) * NY + y
    lat_slot = lat_in.at[lax.rem(z, OPL)]
    lat_copy = remote(
        lat_hbm, lat_slot, send_sem.at[8], recv_sem.at[8], {"cfg": cfg, "seq": taker}
    )

    @pl.when(sends_lat)
    def _():
        lat_copy.start()

    @pl.when(keeps)
    def _():
        pltpu.make_async_copy(lat_hbm, lat_slot, recv_sem.at[8]).start()

    @pl.when(finishes)
    def _():
        for copy in copies:
            copy.wait()
        mod_copy.start()

    lane = lax.broadcasted_iota(jnp.int32, (1, HEAD_DIM), 1)

    @pl.when(attends)
    def _():
        wait_bytes(k_all, recv_sem.at[0])
        wait_bytes(kt_all, recv_sem.at[1])
        wait_bytes(q_all, recv_sem.at[2])
        inv_root = 1.0 / math.sqrt(HEAD_DIM)
        rate = inv_root * math.log2(math.e)
        keys_image = k_all[...].reshape(SEQ * ROWS, HEAD_DIM)
        keys_text = kt_all[...].reshape(SEQ * TROWS, HEAD_DIM)
        position = lax.broadcasted_iota(jnp.int32, (1, SEQ * TROWS), 1)
        usable = position < len_ref[...]
        weights = []
        top = None
        for start in range(0, OWNERS, CHUNK):
            q = q_all[start : start + CHUNK].reshape(CHUNK * ROWS, HEAD_DIM)
            image = nt_dot(q, keys_image)
            text = jnp.where(usable, nt_dot(q, keys_text), -jnp.inf)
            peak = jnp.maximum(
                jnp.max(image, axis=1, keepdims=True), jnp.max(text, axis=1, keepdims=True)
            )
            image = jnp.exp2((image - peak) * rate).astype(BF16)
            text = jnp.exp2((text - peak) * rate).astype(BF16)
            weights.append((image, text))
            most = jnp.max(peak, axis=0, keepdims=True)
            top = most if top is None else jnp.maximum(top, most)
        peak_row[...] = jnp.where(lane == cfg * HEADS + my_head, top * inv_root, -jnp.inf)
        ones = jnp.ones((SEQ * ROWS, HEAD_DIM), BF16)
        wait_bytes(v_all, recv_sem.at[3])
        wait_bytes(vt_all, recv_sem.at[7])
        v_image = jnp.concatenate([v_all[...].reshape(SEQ * ROWS, HEAD_DIM), ones], axis=1)
        v_text = jnp.concatenate(
            [vt_all[...].reshape(SEQ * TROWS, HEAD_DIM), ones[: SEQ * TROWS]], axis=1
        )
        for i, (image, text) in enumerate(weights):
            summed = jnp.dot(image, v_image, preferred_element_type=F32) + jnp.dot(
                text, v_text, preferred_element_type=F32
            )
            result = (summed[:, :HEAD_DIM] / summed[:, HEAD_DIM:]).astype(BF16)
            att[i * CHUNK : (i + 1) * CHUNK] = result.reshape(CHUNK, ROWS, HEAD_DIM)

        for dx, xx in zip(FAR_4, xs):
            for dy in reversed(range(QY)):
                at_y = lax.rem(y + dy, QY)
                for plane_z in reversed(range(LZ)):
                    target = ((LFROM + plane_z) * NX + xx) * NY + (block * QY + at_y)
                    for copy_index in (other, cfg):
                        k = copy_index * LZ + plane_z
                        first = ((k * NX + xx) * QY + at_y) * OPL
                        moves = [
                            (5, att.at[pl.ds(first, OPL)], heads_in.at[cfg, my_head]),
                            (9, peak_row, peaks_in.at[cfg, my_head]),
                        ]

                        def away():
                            device = {"cfg": copy_index, "seq": target}
                            for i, src, dst in moves:
                                remote(src, dst, send_sem.at[i], recv_sem.at[i], device).start()

                        def local():
                            for i, src, dst in moves:
                                pltpu.make_async_copy(src, dst, recv_sem.at[i]).start()

                        if dx == 0 and dy == 0 and copy_index is cfg:
                            pl.when(LFROM + plane_z != z)(away)
                            pl.when(LFROM + plane_z == z)(local)
                        else:
                            away()

    @pl.when(finishes)
    def _():
        mod_copy.wait_recv()
        wait_bytes(lat_in, recv_sem.at[8])
        wait_bytes(heads_in, recv_sem.at[5])
        wait_bytes(peaks_in, recv_sem.at[9])
        parts = heads_in[...].astype(F32)
        average = jnp.sum(jnp.sum(parts, axis=1, keepdims=True), axis=4, keepdims=True) / FEAT
        parts = parts - average
        squares = jnp.sum(parts * parts, axis=1, keepdims=True)
        variance = jnp.sum(squares, axis=4, keepdims=True) / FEAT
        factor = lax.rsqrt(variance + 1e-06)
        normed = parts * factor * (1.0 + mod[:, 1][:, :, None]) + mod[:, 0][:, :, None]
        normed = normed.reshape(2, HEADS, OPL * ROWS, HEAD_DIM).astype(BF16)
        normed = jnp.concatenate([normed[:, h] for h in range(HEADS)], axis=2)
        velocity = nt_dot(normed.reshape(2 * OPL * ROWS, FEAT), w_own[...])
        uncond = velocity[OPL * ROWS :]
        guided = uncond + GUIDANCE * (velocity[: OPL * ROWS] - uncond)
        position = jnp.broadcast_to(step_ref[...].astype(F32), (1, CHAN))
        delta = sigma_at(position + 1.0) - sigma_at(position)
        latents = lat_in[...].reshape(OPL * ROWS, CHAN) + delta * guided
        square = jnp.sum(
            jnp.sum(latents * latents, axis=1, keepdims=True), axis=0, keepdims=True
        )
        tops = jnp.max(peaks_in[...].reshape(2 * HEADS, 1, HEAD_DIM), axis=0)
        sums[my_row] = jnp.where(lane == 2 * HEADS, square, tops)
        done = jnp.concatenate([latents, guided], axis=1)
        result[:OPL] = done.reshape(OPL, ROWS, HEAD_DIM)

        def share(base, skip):
            for offset in plane:
                for copy_index in (cfg, other):
                    if skip and offset is plane[-1] and copy_index is cfg:
                        continue
                    remote(
                        sums.at[my_row],
                        sums.at[my_row],
                        send_sem.at[6],
                        recv_sem.at[6],
                        {"cfg": copy_index, "seq": base + offset},
                    ).start()

        share(lax.rem(z + NZ - 1, NZ) * (NX * NY), False)
        share(z * (NX * NY), True)
        for j in range(OPL):
            owner_z = my_group * OPL + j
            for copy_index in (cfg, other):

                def away():
                    device = {"cfg": copy_index, "seq": (owner_z * NX + x) * NY + y}
                    remote(
                        result.at[j], result_in, send_sem.at[10], recv_sem.at[10], device
                    ).start()

                def local():
                    pltpu.make_async_copy(result.at[j], result_in, recv_sem.at[10]).start()

                if copy_index is cfg:
                    pl.when(owner_z != z)(away)
                    pl.when(owner_z == z)(local)
                else:
                    away()

        def step(i, carry):
            share(lax.rem(z + 1 + i, NZ) * (NX * NY), False)
            return carry

        lax.fori_loop(0, NZ - 2, step, 0)

    wait_bytes(result_in, recv_sem.at[10])
    latents = result_in[:, :CHAN]
    guided = result_in[:, CHAN:]
    half = CHAN // 2
    out_ref[0, :, :half] = jnp.where(cfg == 0, latents[:, :half], latents[:, half:])
    out_ref[1, :, :half] = jnp.where(cfg == 0, guided[:, :half], guided[:, half:])

    @pl.when(sends_lat)
    def _():
        lat_copy.wait_send()

    @pl.when(attends)
    def _():
        wait_bytes(k_all.at[: UNITS - 1], send_sem.at[0])
        wait_bytes(kt_all.at[: UNITS - 1], send_sem.at[1])
        wait_bytes(q_all.at[: HEADS - 1], send_sem.at[2])
        wait_bytes(v_all.at[: UNITS - 1], send_sem.at[3])
        wait_bytes(vt_all.at[: UNITS - 1], send_sem.at[7])

    @pl.when(idle)
    def _():
        wait_bytes(k_all.at[:UNITS], send_sem.at[0])
        wait_bytes(kt_all.at[:UNITS], send_sem.at[1])
        wait_bytes(q_all.at[:HEADS], send_sem.at[2])
        wait_bytes(v_all.at[:UNITS], send_sem.at[3])
        wait_bytes(vt_all.at[:UNITS], send_sem.at[7])

    @pl.when(attends & finishes)
    def _():
        wait_bytes(att.at[: OWNERS - OPL], send_sem.at[5])
        wait_bytes(sums.at[: FINAL_BLOCK - 1], send_sem.at[9])

    @pl.when(attends & passes)
    def _():
        wait_bytes(att, send_sem.at[5])
        wait_bytes(sums.at[:FINAL_BLOCK], send_sem.at[9])

    @pl.when(finishes)
    def _():
        mod_copy.wait_send()
        wait_bytes(sums.at[: FINAL - 1], recv_sem.at[6])

    @pl.when(passes)
    def _():
        wait_bytes(sums.at[:FINAL], recv_sem.at[6])

    rows = sums[:FINAL]
    norm = jnp.sqrt(jnp.sum(rows, axis=0) / (SEQ * ROWS * CHAN))
    tops = jnp.max(rows, axis=0)
    out_ref[2, 0:1, :HEADS] = jnp.where(cfg == 0, tops[:, :HEADS], tops[:, HEADS : 2 * HEADS])
    out_ref[2, 1:2, :] = norm

    @pl.when(finishes)
    def _():
        wait_bytes(sums.at[: 2 * SEQ - 1], send_sem.at[6])

    @pl.when(finishes & keeps)
    def _():
        wait_bytes(result.at[: 2 * OPL - 1], send_sem.at[10])

    @pl.when(finishes & jnp.logical_not(keeps))
    def _():
        wait_bytes(result, send_sem.at[10])


def per_device(
    q_image, k_image, v_image, k_text, v_text, text_len, shift, scale, w_latent, latents, step_index
):
    anywhere = pl.BlockSpec(memory_space=pltpu.HBM)
    vmem = pl.BlockSpec(memory_space=pltpu.VMEM)
    half = CHAN // 2
    packed = pl.pallas_call(
        kernel,
        out_shape=pltpu.VMEM((3, ROWS, HEAD_DIM), F32),
        in_specs=[vmem] * 2 + [anywhere] * 9,
        out_specs=vmem,
        scratch_shapes=[
            pltpu.VMEM((ROWS, FEAT), BF16),
            pltpu.VMEM((ROWS, FEAT), BF16),
            pltpu.VMEM((ROWS, FEAT), BF16),
            pltpu.VMEM((TROWS, FEAT), BF16),
            pltpu.VMEM((TROWS, FEAT), BF16),
            pltpu.VMEM((CHAN, FEAT), BF16),
            pltpu.VMEM((OPL, ROWS, CHAN), F32),
            pltpu.VMEM((2, 2, HEADS, 1, HEAD_DIM), F32),
            pltpu.VMEM((OWNERS, ROWS, HEAD_DIM), BF16),
            pltpu.VMEM((SEQ, ROWS, HEAD_DIM), BF16),
            pltpu.VMEM((SEQ, TROWS, HEAD_DIM), BF16),
            pltpu.VMEM((SEQ, ROWS, HEAD_DIM), BF16),
            pltpu.VMEM((SEQ, TROWS, HEAD_DIM), BF16),
            pltpu.VMEM((OWNERS, ROWS, HEAD_DIM), BF16),
            pltpu.VMEM((1, HEAD_DIM), F32),
            pltpu.VMEM((2, HEADS, OPL, ROWS, HEAD_DIM), BF16),
            pltpu.VMEM((2, HEADS, 1, HEAD_DIM), F32),
            pltpu.VMEM((2 * OPL, ROWS, HEAD_DIM), F32),
            pltpu.VMEM((ROWS, HEAD_DIM), F32),
            pltpu.VMEM((2 * SEQ, 1, HEAD_DIM), F32),
            pltpu.SemaphoreType.DMA((8,)),
            pltpu.SemaphoreType.DMA((11,)),
            pltpu.SemaphoreType.DMA((11,)),
        ],
        compiler_params=pltpu.CompilerParams(collective_id=0, has_side_effects=True),
        name="joint_attention_step",
    )(
        text_len,
        step_index.reshape(1, 1),
        q_image,
        k_image,
        v_image,
        k_text,
        v_text,
        shift.reshape(1, HEADS, 1, HEAD_DIM),
        scale.reshape(1, HEADS, 1, HEAD_DIM),
        w_latent.T,
        latents,
    )
    return (
        packed[0, :, :half],
        packed[1, :, :half],
        packed[2, 1, 2 * HEADS : 2 * HEADS + 1],
        packed[2, 0:1, :HEADS].reshape(1, 1, HEADS),
    )


def solution(mesh):
    placed = (
        P("cfg", ("req", "seq"), None),
        P("cfg", ("req", "seq"), None),
        P("cfg", ("req", "seq"), None),
        P("cfg", ("req", "seq"), None),
        P("cfg", ("req", "seq"), None),
        P("cfg", "req"),
        P("cfg", "req", None),
        P("cfg", "req", None),
        P(),
        P(("req", "seq"), None),
        P(),
    )
    return jax.shard_map(
        per_device,
        mesh=mesh,
        in_specs=placed,
        out_specs=(
            P(("req", "seq"), "cfg"),
            P(("req", "seq"), "cfg"),
            P("req"),
            P("cfg", "req", None),
        ),
        check_vma=False,
    )
```
